32 devices in a mesh: grp: 2 (over y), gx: 16 (over z, x, core).
Axes of the slice: x: 2, y: 2, z: 4, core: 2. Of those that a mesh axis runs over, the one named last changes fastest.
Arguments:
- mesh_feature_array: bfloat16 [128, 32, 32, 512], P(('grp', 'gx')), parts along dimension 0, may hold values from -6 to 6
- stencil_coefficients: float32 [27, 512], replicated, may hold values from -1.25 to 1.25
- partition_affinity_matrix: bfloat16 [512, 512], replicated, may hold values from -16 to 16
- softness_mapping_matrix: float32 [512], replicated, may hold values from -0.25 to 0.25
- content_mapping_matrix: bfloat16 [512, 512], replicated, may hold values from -0.25 to 0.25
- layernorm_multiplier: float32 [512], replicated, may hold values from 0.1 to 1.9
- widening_matrix: bfloat16 [512, 1024], replicated, may hold values from -0.25 to 0.25
- narrowing_matrix: bfloat16 [1024, 512], replicated, may hold values from -0.1875 to 0.1875
- final_mapping_matrix: bfloat16 [512, 512], replicated, may hold values from -0.25 to 0.25
Outputs:
- updated: bfloat16 [128, 32, 32, 512], P(('grp', 'gx')), parts along dimension 0
- slice_out: bfloat16 [1024, 512], P(('grp', 'gx')), parts along dimension 0
The draws below stay inside these ranges and needn't reach their ends.
There are 2 independent parts, one for each index of `grp`. The reference program is written for one: setup_inputs(seed, part) draws one part's arguments, and reference() takes and returns one part's arrays. A program takes and returns all parts, laid end to end along the dimension named above; an argument that names none is the same for every part. Nothing has to cross between parts.
All inputs are finite; a program needn't handle non-finite values.
Results may differ from the reference program's by a relative error of at most 0.0056.
Values may be sent and summed in bfloat16 or wider, within the bound.
A program may use at most 128 MiB of HBM per device.

```python
import math
import jax
import jax.numpy as jnp
from jax import lax

CHANNEL_COUNT = 512
M = 512
HID = 1024
NY = 32
NZ = 32
NX = 64


def draw_partition_affinity_matrix(key, part):
    key = jax.random.fold_in(key, 7)
    key_base = jax.random.fold_in(key, 0)
    base = jax.random.normal(key_base, (CHANNEL_COUNT, M), jnp.float32) * (3.0 / math.sqrt(CHANNEL_COUNT))
    return jnp.clip(base, -16.0, 16.0).astype(jnp.bfloat16)


def block_scale(rng, shape, cuts, low, top_value):
    loudness = 1.0
    for dim, blocks in cuts:
        steps = jax.random.uniform(jax.random.fold_in(jax.random.fold_in(rng, 6), dim), (blocks,), jnp.float32, low / len(cuts), top_value / len(cuts))
        loudness = loudness * jnp.repeat(jnp.exp(steps), shape[dim] // blocks).reshape((-1,) + (1,) * (len(shape) - 1 - dim))
    return loudness


def gaussian(rng, dims, width, most, pieces=(), dtype=jnp.bfloat16):
    loudness = block_scale(rng, dims, pieces, -0.22, 0.18) if pieces else 1.0
    drawn = jax.random.normal(rng, dims, jnp.float32) * width * loudness
    return jnp.minimum(jnp.maximum(drawn, -most), most).astype(dtype)


def setup_inputs(seed: int = 0, part: int = 0) -> dict:
    arg_keys = jax.random.split(jax.random.key(seed), 10)
    part_splits = jax.random.split(jax.random.fold_in(arg_keys[9], part), 10)
    mesh_feature_array = gaussian(part_splits[0], (NX, NY, NZ, CHANNEL_COUNT), 1.0, 6.0, ((0, 16),))
    stencil_coefficients = gaussian(arg_keys[1], (27, CHANNEL_COUNT), 27 ** -0.5, 1.25, (), jnp.float32)
    partition_affinity_matrix = draw_partition_affinity_matrix(jax.random.fold_in(arg_keys[9], 71), part)
    softness_mapping_matrix = gaussian(arg_keys[3], (CHANNEL_COUNT,), CHANNEL_COUNT ** -0.5, 0.25, (), jnp.float32)
    content_mapping_matrix = gaussian(arg_keys[4], (CHANNEL_COUNT, CHANNEL_COUNT), CHANNEL_COUNT ** -0.5, 0.25)
    layernorm_multiplier = jnp.clip(1.0 + 0.18 * jax.random.normal(arg_keys[5], (CHANNEL_COUNT,), jnp.float32), 0.1, 1.9)
    widening_matrix = gaussian(arg_keys[6], (CHANNEL_COUNT, HID), CHANNEL_COUNT ** -0.5, 0.25)
    narrowing_matrix = gaussian(arg_keys[7], (HID, CHANNEL_COUNT), HID ** -0.5, 0.1875)
    final_mapping_matrix = gaussian(arg_keys[8], (CHANNEL_COUNT, CHANNEL_COUNT), CHANNEL_COUNT ** -0.5, 0.25)
    return {"mesh_feature_array": mesh_feature_array, "stencil_coefficients": stencil_coefficients, "partition_affinity_matrix": partition_affinity_matrix, "softness_mapping_matrix": softness_mapping_matrix, "content_mapping_matrix": content_mapping_matrix, "layernorm_multiplier": layernorm_multiplier, "widening_matrix": widening_matrix, "narrowing_matrix": narrowing_matrix, "final_mapping_matrix": final_mapping_matrix}


epsilon = 1e-05

def conv_gelu(padded, stencil_coefficients, size_x, size_y, size_z):
    total = jnp.zeros((size_x, size_y, size_z, stencil_coefficients.shape[1]), jnp.float32)
    for offset_a in range(3):
        for offset_b in range(3):
            for offset_c in range(3):
                window = padded[offset_a:offset_a + size_x, offset_b:offset_b + size_y, offset_c:offset_c + size_z]
                total = total + window.astype(jnp.float32) * stencil_coefficients[9 * offset_a + 3 * offset_b + offset_c]
    return jax.nn.gelu(total).astype(jnp.bfloat16)

def owner_mlp(tokens, layernorm_multiplier, widening_matrix, narrowing_matrix):
    center = lax.optimization_barrier(jnp.mean(tokens, axis=-1, keepdims=True))
    spread = lax.optimization_barrier(jnp.mean((tokens - center) ** 2, axis=-1, keepdims=True))
    normed = ((tokens - center) * lax_rsqrt(spread + epsilon) * layernorm_multiplier).astype(jnp.bfloat16)
    inner = jax.nn.gelu(jnp.dot(normed, widening_matrix, preferred_element_type=jnp.float32)).astype(jnp.bfloat16)
    return (tokens + jnp.dot(inner, narrowing_matrix, preferred_element_type=jnp.float32)).astype(jnp.bfloat16)

def lax_rsqrt(value):
    return 1.0 / jnp.sqrt(value)

def reference(mesh_feature_array, stencil_coefficients, partition_affinity_matrix, softness_mapping_matrix, content_mapping_matrix, layernorm_multiplier, widening_matrix, narrowing_matrix, final_mapping_matrix):
    padded = jnp.pad(mesh_feature_array, ((1, 1), (1, 1), (1, 1), (0, 0)))
    intermediate_response = conv_gelu(padded, stencil_coefficients, NX, NY, NZ).reshape(-1, CHANNEL_COUNT)
    local_softness_factor = 0.25 + jax.nn.softplus(jnp.dot(intermediate_response, softness_mapping_matrix.astype(jnp.bfloat16), preferred_element_type=jnp.float32))
    partition_affinity_raw = jnp.dot(intermediate_response, partition_affinity_matrix, preferred_element_type=jnp.float32) / local_softness_factor[:, None]
    slice_probs = jax.nn.softmax(partition_affinity_raw, axis=-1).astype(jnp.bfloat16)
    values = jnp.dot(intermediate_response, content_mapping_matrix, preferred_element_type=jnp.float32).astype(jnp.bfloat16)
    weighted_tokens = jax.lax.dot_general(slice_probs, values, (((0,), (0,)), ((), ())), preferred_element_type=jnp.float32)
    mass = lax.optimization_barrier(jnp.sum(slice_probs.astype(jnp.float32), axis=0))
    tokens = weighted_tokens / (mass[:, None] + epsilon)
    slice_out = owner_mlp(tokens, layernorm_multiplier, widening_matrix, narrowing_matrix)
    desliced = jnp.dot(slice_probs, slice_out, preferred_element_type=jnp.float32).astype(jnp.bfloat16)
    flat = mesh_feature_array.reshape(-1, CHANNEL_COUNT).astype(jnp.float32)
    updated = (flat + jnp.dot(desliced, final_mapping_matrix, preferred_element_type=jnp.float32)).astype(jnp.bfloat16)
    return (updated.reshape(NX, NY, NZ, CHANNEL_COUNT), slice_out)
```

```python
import functools
import math

import jax
import jax.numpy as jnp
from jax import lax
from jax.experimental import pallas as pl
from jax.experimental.pallas import tpu as pltpu
from jax.sharding import PartitionSpec as P

epsilon = 1e-05
MESH = pl.DeviceIdType.MESH
F32 = jnp.float32
BF16 = jnp.bfloat16
LANES = 128
MIB = 1024 * 1024
SLAB_LIMIT = 32 * MIB
SMALL_LIMIT = 12 * MIB
OFFSETS = (-1, 1, 0, 0)
TERMS = (
    [(a, b, 0) for a in range(3) for b in range(3)],
    [(a, b, 2) for a in range(3) for b in range(3)],
    [(a, b, 1) for a in range(2) for b in range(3)],
    [(2, b, 1) for b in range(3)],
)


def gelu(v):
    a = math.sqrt(2.0 / math.pi)
    return 0.5 * v * (1.0 + jnp.tanh(v * (a + (a * 0.044715) * (v * v))))


CONV_ROWS = 4
CHUNK_ROWS = 8
LOG2E = math.log2(math.e)


def slab_kernel(
    n, x_ref, taps_hbm, aff_hbm, soft_hbm, prob, g_out,
    taps_ref, aff_ref, soft_ref, pad, taps, aug, shift, hid_a, hid_b, logit, probt, acc, macc,
    load_sem, small_sem, send_sem, recv_sem,
):
    planes, rows_y, rows_z, channels = x_ref.shape
    slices = aff_ref.shape[1]
    chunk_rows = CHUNK_ROWS
    chunk = chunk_rows * rows_z
    per_plane = rows_y // chunk_rows
    steps = planes * per_plane
    me = lax.axis_index("gx")
    inside = pl.ds(1, rows_y)
    has_left, has_right = me > 0, me < n - 1
    core, early = lax.rem(me, 2), max(planes - 2, 0)

    small = []
    for i, (src, dst) in enumerate(
        ((taps_hbm, taps_ref), (aff_hbm, aff_ref), (soft_hbm, soft_ref))
    ):
        copy = pltpu.make_async_copy(src, dst, small_sem.at[i])
        copy.start()
        small.append(copy)
    loads = []
    for j in range(planes):
        copy = pltpu.make_async_copy(x_ref.at[j], pad.at[j + 1, inside], load_sem.at[j])
        copy.start()
        loads.append(copy)

    barrier = pltpu.get_barrier_semaphore()

    @pl.when(has_left)
    def _():
        pl.semaphore_signal(barrier, inc=1, device_id={"gx": me - 1}, device_id_type=MESH)

    @pl.when(has_right)
    def _():
        pl.semaphore_signal(barrier, inc=1, device_id={"gx": me + 1}, device_id_type=MESH)

    pl.semaphore_wait(barrier, jnp.minimum(me, 1) + jnp.minimum(n - 1 - me, 1))

    ends = [min((k + 1) * chunk_rows + 1, rows_y) for k in range(per_plane)]
    up, down = [], []
    for k, (lo, hi) in enumerate(zip([0] + ends[:-1], ends)):
        up.append(
            pltpu.make_async_remote_copy(
                src_ref=x_ref.at[planes - 1, pl.ds(lo, hi - lo)],
                dst_ref=pad.at[0, pl.ds(1 + lo, hi - lo)],
                send_sem=send_sem.at[0, k], recv_sem=recv_sem.at[0, k],
                device_id={"gx": me + 1}, device_id_type=MESH,
            )
        )
        down.append(
            pltpu.make_async_remote_copy(
                src_ref=x_ref.at[0, pl.ds(lo, hi - lo)],
                dst_ref=pad.at[planes + 1, pl.ds(1 + lo, hi - lo)],
                send_sem=send_sem.at[1, k], recv_sem=recv_sem.at[1, k],
                device_id={"gx": me - 1}, device_id_type=MESH,
            )
        )

    @pl.when(has_right)
    def _():
        for copy in up:
            copy.start()

    @pl.when(has_left)
    def _():
        for copy in down:
            copy.start()

    for i in range(planes + 2):
        pad[i, 0] = jnp.zeros((rows_z, channels), BF16)
        pad[i, rows_y + 1] = jnp.zeros((rows_z, channels), BF16)

    @pl.when(jnp.logical_not(has_left))
    def _():
        pad[0, inside] = jnp.zeros((rows_y, rows_z, channels), BF16)

    @pl.when(jnp.logical_not(has_right))
    def _():
        pad[planes + 1, inside] = jnp.zeros((rows_y, rows_z, channels), BF16)

    acc[...] = jnp.zeros_like(acc)
    macc[...] = jnp.zeros_like(macc)
    r = lax.broadcasted_iota(jnp.int32, shift.shape, 0)
    k = lax.broadcasted_iota(jnp.int32, shift.shape, 1)
    block = lax.rem(k // rows_z, len(OFFSETS))
    off = jnp.zeros_like(k)
    for j, o in enumerate(OFFSETS):
        off = jnp.where(block == j, o, off)
    hit = jnp.logical_and(
        k // (rows_z * len(OFFSETS)) == r // rows_z,
        lax.rem(k, rows_z) == lax.rem(r, rows_z) + off,
    )
    shift[...] = jnp.where(hit, 1.0, 0.0).astype(BF16)
    for copy in small:
        copy.wait()
    for t in range(27):
        taps[t] = jnp.broadcast_to(0.5 * taps_ref[t : t + 1, :], taps.shape[1:]).astype(BF16)
    aug[:slices, :] = aff_ref[...].T
    aug[slices:, :] = jnp.broadcast_to(soft_ref[...], (aug.shape[0] - slices, channels)).astype(BF16)
    for copy in loads[:3]:
        copy.wait()

    def where(s):
        i, part = s // per_plane, lax.rem(s, per_plane)
        p = jnp.where(i < planes - 2, i + 1, jnp.where((i == planes - 1) == (core == 0), 0, planes - 1))
        return p, part

    first_up = jnp.where(core == 0, planes - 1, early) * per_plane
    first_down = jnp.where(core == 0, early, planes - 1) * per_plane

    def arrive(*chunks):
        @pl.when(chunks[-1] == min(1, planes - 1) * per_plane)
        def _():
            for copy in loads[3:]:
                copy.wait()

        @pl.when(chunks[-1] >= early * per_plane)
        def _():
            for s in chunks:
                for k in range(per_plane):

                    @pl.when(jnp.logical_and(s == first_up + k, has_left))
                    def _():
                        up[k].wait_recv()

                    @pl.when(jnp.logical_and(s == first_down + k, has_right))
                    def _():
                        down[k].wait_recv()

    def conv_unit(p, y, local, lanes, hid):
        halves = []
        for base in range(lanes.start, lanes.stop, LANES):
            cs = slice(base, base + LANES)
            v = [[pad[p + a, y + b, :, cs] for b in range(CONV_ROWS + 2)] for a in range(3)]
            rows = []
            for q in range(CONV_ROWS):
                blocks = []
                for terms in TERMS:
                    total = None
                    for a, b, c in terms:
                        tap = taps[9 * a + 3 * b + c, :, cs]
                        tap = jnp.concatenate([tap] * (rows_z // tap.shape[0]), axis=0)
                        t = tap * v[a][q + b]
                        total = t if total is None else total + t
                    blocks.append(total)
                rows.append(blocks)
            halves.append(rows)
        per = shift.shape[0] // rows_z
        for q in range(0, CONV_ROWS, per):
            operand = jnp.concatenate(
                [
                    jnp.concatenate([t for row in rows[q : q + per] for t in row], axis=0)
                    for rows in halves
                ],
                axis=1,
            )
            h = jnp.dot(shift[...], operand, preferred_element_type=F32)
            a = math.sqrt(2.0 / math.pi)
            u = h * (2 * a + (8 * a * 0.044715) * (h * h))
            hid[(local + q) * rows_z : (local + q + per) * rows_z, lanes] = (
                h + h * jnp.tanh(u)
            ).astype(BF16)

    def units(s, hid):
        if s is None:
            return [lambda: None] * 4
        p, part = where(s)
        out = []
        for local in range(0, chunk_rows, CONV_ROWS):
            for base in range(0, channels, 2 * LANES):
                out.append(
                    functools.partial(
                        conv_unit, p, part * chunk_rows + local, local, slice(base, base + 2 * LANES), hid
                    )
                )
        return out

    def soft_stages(s, hid):
        if s is None:
            return [lambda: None] * 4
        p, part = where(s)
        state = {}

        def logits():
            lt = lax.dot_general(aug[...], hid[...], (((1,), (1,)), ((), ())), preferred_element_type=F32)
            z = lt[slices : slices + 8]
            temp = 0.25 + jnp.maximum(z, 0.0) + jnp.log(1.0 + jnp.exp(-jnp.abs(z)))
            state["rate"] = LOG2E / temp
            logit[...] = lt[:slices]
            state["top"] = jnp.max(lt[:slices].reshape(slices // 8, 8, chunk), axis=0)

        def powers():
            top = jnp.broadcast_to(jnp.max(state["top"], axis=0, keepdims=True), (8, chunk))
            rate = state["rate"]
            total = None
            for j in range(0, slices, 8):
                e = jnp.exp2((logit[j : j + 8, :] - top) * rate)
                logit[j : j + 8, :] = e
                total = e if total is None else total + e
            state["sum"] = total

        def scale():
            total = jnp.sum(state["sum"], axis=0, keepdims=True)
            inverse = jnp.broadcast_to(1.0 / total, (16, chunk))
            for j in range(0, slices, 16):
                probt[j : j + 16, :] = (logit[j : j + 16, :] * inverse).astype(BF16)

        def gather():
            acc[...] += jnp.dot(probt[...], hid[...], preferred_element_type=F32)
            ones = jnp.ones((16, chunk), BF16)
            macc[...] += lax.dot_general(
                ones, probt[...], (((1,), (1,)), ((), ())), preferred_element_type=F32
            )
            rs = pl.ds(pl.multiple_of(part * chunk, chunk), chunk)
            for j in range(0, slices, LANES):
                prob[p, rs, j : j + LANES] = probt[j : j + LANES, :].T

        return [logits, powers, scale, gather]

    def step(sc, hid_c, ss, hid_s):
        for soft, conv in zip(soft_stages(ss, hid_s), units(sc, hid_c)):
            soft()
            conv()

    step(0, hid_a, None, None)

    def body(u, carry):
        arrive(2 * u + 1, 2 * u + 2)
        step(2 * u + 1, hid_b, 2 * u, hid_a)
        step(2 * u + 2, hid_a, 2 * u + 1, hid_b)
        return carry

    lax.fori_loop(0, steps // 2 - 1, body, 0)
    step(None, None, steps - 2, hid_a)
    arrive(steps - 1)
    step(steps - 1, hid_b, None, None)
    step(None, None, steps - 1, hid_b)

    g_out[:, :channels] = acc[...].astype(BF16)
    mass = jnp.broadcast_to(macc[:1, :], (LANES, slices)).T
    high = mass.astype(BF16).astype(F32)
    lane = lax.broadcasted_iota(jnp.int32, (slices, LANES), 1)
    g_out[:, channels:] = jnp.where(lane < LANES // 2, high, mass - high).astype(BF16)

    @pl.when(has_right)
    def _():
        for copy in up:
            copy.wait_send()

    @pl.when(has_left)
    def _():
        for copy in down:
            copy.wait_send()


def slab(n, x, taps, aff, soft):
    planes, rows_y, rows_z, channels = x.shape
    slices = aff.shape[1]
    cells = rows_y * rows_z
    chunk = CHUNK_ROWS * rows_z
    depth = len(OFFSETS) * rows_z
    per_plane = rows_y // CHUNK_ROWS
    per = max(256 // depth, 1)
    vmem_spec = pl.BlockSpec(memory_space=pltpu.VMEM)
    dma = pltpu.SemaphoreType.DMA
    return pl.pallas_call(
        functools.partial(slab_kernel, n),
        out_shape=(
            jax.ShapeDtypeStruct((planes, cells, slices), BF16),
            jax.ShapeDtypeStruct((slices, channels + LANES), BF16),
        ),
        in_specs=[pl.BlockSpec(memory_space=pltpu.HBM)] * 4,
        out_specs=(vmem_spec, vmem_spec),
        scratch_shapes=[
            pltpu.VMEM(taps.shape, F32),
            pltpu.VMEM(aff.shape, BF16),
            pltpu.VMEM(soft.shape, F32),
            pltpu.VMEM((planes + 2, rows_y + 2, rows_z, channels), BF16),
            pltpu.VMEM((27, 16, channels), BF16),
            pltpu.VMEM((slices + 16, channels), BF16),
            pltpu.VMEM((per * rows_z, per * depth), BF16),
            pltpu.VMEM((chunk, channels), BF16),
            pltpu.VMEM((chunk, channels), BF16),
            pltpu.VMEM((slices, chunk), F32),
            pltpu.VMEM((slices, chunk), BF16),
            pltpu.VMEM((slices, channels), F32),
            pltpu.VMEM((16, slices), F32),
            dma((planes,)),
            dma((3,)),
            dma((2, per_plane)),
            dma((2, per_plane)),
        ],
        compiler_params=pltpu.CompilerParams(
            collective_id=1, has_side_effects=True, vmem_limit_bytes=SLAB_LIMIT
        ),
        name="slab",
    )(x, taps, aff, soft)


def exchange_kernel(
    n,
    g_ref,
    gain_hbm,
    wc_hbm,
    w1_hbm,
    w2_hbm,
    wf_hbm,
    own_ref,
    all_ref,
    gain_ref,
    wc,
    w1,
    w2,
    wf,
    pair_in,
    summed,
    ring_in,
    w_sem,
    s1,
    r1,
    s2,
    r2,
    s3,
    r3,
    s4,
    r4,
):
    me = lax.axis_index("gx")
    half = n // 2
    core = lax.rem(me, 2)
    chip = me // 2
    partner = me + 1 - 2 * core
    channels = wc.shape[0]

    def there(d):
        return 2 * lax.rem(chip + d, half) + core

    def origin(d):
        return lax.rem(chip + half - d, half)

    loads = []
    for i, (src, dst) in enumerate(
        ((wc_hbm, wc), (w1_hbm, w1), (w2_hbm, w2), (wf_hbm, wf), (gain_hbm, gain_ref))
    ):
        copy = pltpu.make_async_copy(src, dst, w_sem.at[i])
        copy.start()
        loads.append(copy)

    barrier = pltpu.get_barrier_semaphore()
    pl.semaphore_signal(barrier, inc=1, device_id={"gx": partner}, device_id_type=MESH)
    for d in range(1, half):
        pl.semaphore_signal(barrier, inc=1, device_id={"gx": there(d)}, device_id_type=MESH)
    pl.semaphore_wait(barrier, half)

    def remote(src, dst, ss, rs, to):
        return pltpu.make_async_remote_copy(
            src_ref=src, dst_ref=dst, send_sem=ss, recv_sem=rs,
            device_id={"gx": to}, device_id_type=MESH,
        )

    pair = []
    for d in range(half):
        k = lax.rem(chip + (d + 1) % half, half)
        copy = remote(g_ref.at[k, 1 - core], pair_in.at[k], s1.at[d], r1.at[d], partner)
        copy.start()
        pair.append(copy)
    sends = []
    for d in range(1, half):
        k = lax.rem(chip + d, half)
        pair[d - 1].wait_recv()
        summed[k] = (g_ref[k, core].astype(F32) + pair_in[k].astype(F32)).astype(BF16)
        copy = remote(summed.at[k], ring_in.at[d], s2.at[d], r2.at[d], there(d))
        copy.start()
        sends.append(copy)
    pair[half - 1].wait_recv()
    acc = g_ref[chip, core].astype(F32) + pair_in[chip].astype(F32)
    for d in range(1, half):
        sends[d - 1].wait_recv()
        acc = acc + ring_in[d].astype(F32)
    for copy in loads:
        copy.wait()

    mass = acc[:, channels : channels + 1] + acc[
        :, channels + LANES // 2 : channels + LANES // 2 + 1
    ]
    mean_hidden = acc[:, :channels] / (mass + epsilon)
    high = mean_hidden.astype(BF16)
    low = (mean_hidden - high.astype(F32)).astype(BF16)
    tokens = jnp.dot(high, wc[...], preferred_element_type=F32) + jnp.dot(
        low, wc[...], preferred_element_type=F32
    )
    center = jnp.mean(tokens, axis=-1, keepdims=True)
    spread = jnp.mean((tokens - center) ** 2, axis=-1, keepdims=True)
    normed = ((tokens - center) * (1.0 / jnp.sqrt(spread + epsilon)) * gain_ref[...]).astype(BF16)
    inner = gelu(jnp.dot(normed, w1[...], preferred_element_type=F32)).astype(BF16)
    own = (tokens + jnp.dot(inner, w2[...], preferred_element_type=F32)).astype(BF16)
    own_ref[...] = own
    all_ref[me] = jnp.dot(own, wf[...], preferred_element_type=F32).astype(BF16)

    out = []
    for d in range(1, half):
        copy = remote(all_ref.at[me], all_ref.at[me], s3.at[d], r3.at[d], there(d))
        copy.start()
        out.append(copy)
    first = remote(all_ref.at[me], all_ref.at[me], s4.at[0], r4.at[0], partner)
    first.start()
    relays = [first]
    for d in range(1, half):
        out[d - 1].wait_recv()
        block = 2 * origin(d) + core
        copy = remote(all_ref.at[block], all_ref.at[block], s4.at[d], r4.at[d], partner)
        copy.start()
        relays.append(copy)
    for copy in pair + sends + out:
        copy.wait_send()
    for copy in relays:
        copy.wait()


def exchange(n, g, gain, wc, w1, w2, wf):
    slices, width = g.shape
    channels = wc.shape[0]
    rows, half = slices // n, n // 2
    vmem_spec = pl.BlockSpec(memory_space=pltpu.VMEM)
    dma = pltpu.SemaphoreType.DMA
    return pl.pallas_call(
        functools.partial(exchange_kernel, n),
        out_shape=(
            jax.ShapeDtypeStruct((rows, channels), BF16),
            jax.ShapeDtypeStruct((n, rows, channels), BF16),
        ),
        in_specs=[vmem_spec] + [pl.BlockSpec(memory_space=pltpu.HBM)] * 5,
        out_specs=(vmem_spec, vmem_spec),
        scratch_shapes=[
            pltpu.VMEM(gain.shape, F32),
            pltpu.VMEM(wc.shape, BF16),
            pltpu.VMEM(w1.shape, BF16),
            pltpu.VMEM(w2.shape, BF16),
            pltpu.VMEM(wf.shape, BF16),
            pltpu.VMEM((half, rows, width), BF16),
            pltpu.VMEM((half, rows, width), BF16),
            pltpu.VMEM((half, rows, width), BF16),
            dma((5,)),
        ]
        + [dma((half,))] * 8,
        compiler_params=pltpu.CompilerParams(
            collective_id=0, has_side_effects=True, vmem_limit_bytes=SMALL_LIMIT
        ),
        name="exchange",
    )(g.reshape(half, 2, rows, width), gain, wc, w1, w2, wf)


def final_kernel(x_ref, p_ref, f_ref, own_ref, o_hbm, own_out, buf, sem):
    own_out[...] = own_ref[...]
    slots, block, _ = buf.shape
    steps = x_ref.shape[0] // block
    out = []
    for i in range(steps):
        rs = pl.ds(i * block, block)
        if i >= slots:
            out[i - slots].wait()
        buf[i % slots] = (
            x_ref[rs, :].astype(F32)
            + jnp.dot(p_ref[rs, :], f_ref[...], preferred_element_type=F32)
        ).astype(BF16)
        copy = pltpu.make_async_copy(buf.at[i % slots], o_hbm.at[rs, :], sem.at[i % slots])
        copy.start()
        out.append(copy)
    for copy in out[max(steps - slots, 0) :]:
        copy.wait()


def final(x, p, f, own):
    cells, channels = x.shape
    block = math.gcd(cells, 512)
    vmem_spec = pl.BlockSpec(memory_space=pltpu.VMEM)
    return pl.pallas_call(
        final_kernel,
        out_shape=(
            jax.ShapeDtypeStruct((cells, channels), BF16),
            jax.ShapeDtypeStruct(own.shape, BF16),
        ),
        in_specs=[vmem_spec] * 4,
        out_specs=(pl.BlockSpec(memory_space=pl.ANY), vmem_spec),
        scratch_shapes=[
            pltpu.VMEM((3, block, channels), BF16),
            pltpu.SemaphoreType.DMA((3,)),
        ],
        compiler_params=pltpu.CompilerParams(vmem_limit_bytes=SMALL_LIMIT),
        name="final",
    )(x, p, f, own)


def per_device(x, stencil, aff, softness, wc, gain, w1, w2, wf):
    planes, rows_y, rows_z, channels = x.shape
    n = lax.axis_size("gx")
    def held(v):
        return pltpu.with_memory_space_constraint(v, pltpu.HBM)

    probs, g = slab(n, held(x), held(stencil), held(aff), held(softness.reshape(1, -1)))
    own, folded = exchange(
        n, g, held(gain.reshape(1, -1)), held(wc), held(w1), held(w2), held(wf)
    )
    updated, own = final(
        x.reshape(-1, channels),
        probs.reshape(planes * rows_y * rows_z, -1),
        folded.reshape(-1, channels),
        own,
    )
    return updated.reshape(x.shape), own


def solution(mesh):
    return jax.shard_map(
        per_device,
        mesh=mesh,
        in_specs=(P(("grp", "gx"), None, None, None), P(), P(), P(), P(), P(), P(), P(), P()),
        out_specs=(P(("grp", "gx"), None, None, None), P(("grp", "gx"), None)),
        check_vma=False,
    )
```

```python
import functools
import math

import jax
import jax.numpy as jnp
from jax import lax
from jax.experimental import pallas as pl
from jax.experimental.pallas import tpu as pltpu
from jax.sharding import PartitionSpec as P

epsilon = 1e-05
MESH = pl.DeviceIdType.MESH
F32 = jnp.float32
BF16 = jnp.bfloat16
LANES = 128
MIB = 1024 * 1024
SLAB_LIMIT = 32 * MIB
SMALL_LIMIT = 12 * MIB
OFFSETS = (-1, -1, -1, 1, 1, 1, 0, 0)
TERMS = (
    [[(a, b, 0) for b in range(3)] for a in range(3)]
    + [[(a, b, 2) for b in range(3)] for a in range(3)]
    + [[(a, b, 1) for a in range(2) for b in range(3)], [(2, b, 1) for b in range(3)]]
)


def gelu(v):
    a = math.sqrt(2.0 / math.pi)
    return 0.5 * v * (1.0 + jnp.tanh(v * (a + (a * 0.044715) * (v * v))))


CONV_ROWS = 4
CHUNK_ROWS = 8
LOG2E = math.log2(math.e)


def slab_kernel(
    n, x_ref, taps_hbm, aff_hbm, soft_hbm, gain_hbm, wc_hbm, w1_hbm, w2_hbm, wf_hbm,
    prob, x_keep, own_ref, all_ref,
    taps_ref, aff_ref, soft_ref, pad, taps, aug, shift, hid_a, hid_b, logit, probt, acc, macc,
    gain_ref, wc, w1, w2, wf, g_ref, pair_in, half_sum, mine, x_in, quarter, z_in,
    load_sem, small_sem, late_sem, send_sem, recv_sem, s1, r1, s2, r2, s3, r3, s4, r4, s5, r5, s6, r6,
):
    planes, rows_y, rows_z, channels = x_ref.shape
    slices = aff_ref.shape[1]
    chunk_rows = CHUNK_ROWS
    chunk = chunk_rows * rows_z
    per_plane = rows_y // chunk_rows
    steps = planes * per_plane
    me = lax.axis_index("gx")
    inside = pl.ds(1, rows_y)
    has_left, has_right = me > 0, me < n - 1
    core, early = lax.rem(me, 2), max(planes - 2, 0)

    count = n // 4
    row, side = me // 4, lax.rem(me // 2, 2)
    partner = me + 1 - 2 * core
    beside = me + 2 - 4 * side

    def ahead(d):
        return lax.rem(row + d, count)

    def behind(d):
        return lax.rem(row + count - d, count)

    def device(q):
        return (2 * q + side) * 2 + core

    barrier = pltpu.get_barrier_semaphore()

    @pl.when(has_left)
    def _():
        pl.semaphore_signal(barrier, inc=1, device_id={"gx": me - 1}, device_id_type=MESH)

    @pl.when(has_right)
    def _():
        pl.semaphore_signal(barrier, inc=1, device_id={"gx": me + 1}, device_id_type=MESH)

    pl.semaphore_signal(barrier, inc=1, device_id={"gx": beside}, device_id_type=MESH)
    for d in range(1, count):
        pl.semaphore_signal(barrier, inc=1, device_id={"gx": device(ahead(d))}, device_id_type=MESH)

    small = []
    for i, (src, dst) in enumerate(
        ((taps_hbm, taps_ref), (aff_hbm, aff_ref), (soft_hbm, soft_ref))
    ):
        copy = pltpu.make_async_copy(src, dst, small_sem.at[i])
        copy.start()
        small.append(copy)
    loads = []
    for j in range(planes):
        copy = pltpu.make_async_copy(x_ref.at[j], pad.at[j + 1, inside], load_sem.at[j])
        copy.start()
        loads.append(copy)
    late = [
        pltpu.make_async_copy(src, dst, late_sem.at[i])
        for i, (src, dst) in enumerate(
            ((x_ref, x_keep), (wc_hbm, wc), (w1_hbm, w1), (w2_hbm, w2), (wf_hbm, wf), (gain_hbm, gain_ref))
        )
    ]

    pl.semaphore_wait(barrier, jnp.minimum(me, 1) + jnp.minimum(n - 1 - me, 1) + count)

    ends = [min((k + 1) * chunk_rows + 1, rows_y) for k in range(per_plane)]
    up, down = [], []
    for k, (lo, hi) in enumerate(zip([0] + ends[:-1], ends)):
        up.append(
            pltpu.make_async_remote_copy(
                src_ref=x_ref.at[planes - 1, pl.ds(lo, hi - lo)],
                dst_ref=pad.at[0, pl.ds(1 + lo, hi - lo)],
                send_sem=send_sem.at[0, k], recv_sem=recv_sem.at[0, k],
                device_id={"gx": me + 1}, device_id_type=MESH,
            )
        )
        down.append(
            pltpu.make_async_remote_copy(
                src_ref=x_ref.at[0, pl.ds(lo, hi - lo)],
                dst_ref=pad.at[planes + 1, pl.ds(1 + lo, hi - lo)],
                send_sem=send_sem.at[1, k], recv_sem=recv_sem.at[1, k],
                device_id={"gx": me - 1}, device_id_type=MESH,
            )
        )

    @pl.when(has_right)
    def _():
        for copy in up:
            copy.start()

    @pl.when(has_left)
    def _():
        for copy in down:
            copy.start()

    for i in range(planes + 2):
        pad[i, 0] = jnp.zeros((rows_z, channels), BF16)
        pad[i, rows_y + 1] = jnp.zeros((rows_z, channels), BF16)

    @pl.when(jnp.logical_not(has_left))
    def _():
        pad[0, inside] = jnp.zeros((rows_y, rows_z, channels), BF16)

    @pl.when(jnp.logical_not(has_right))
    def _():
        pad[planes + 1, inside] = jnp.zeros((rows_y, rows_z, channels), BF16)

    acc[...] = jnp.zeros_like(acc)
    macc[...] = jnp.zeros_like(macc)
    r = lax.broadcasted_iota(jnp.int32, shift.shape, 0)
    k = lax.broadcasted_iota(jnp.int32, shift.shape, 1)
    block = lax.rem(k // rows_z, len(OFFSETS))
    off = jnp.zeros_like(k)
    for j, o in enumerate(OFFSETS):
        off = jnp.where(block == j, o, off)
    hit = jnp.logical_and(
        k // (rows_z * len(OFFSETS)) == r // rows_z,
        lax.rem(k, rows_z) == lax.rem(r, rows_z) + off,
    )
    shift[...] = jnp.where(hit, 1.0, 0.0).astype(BF16)
    for copy in small:
        copy.wait()
    for t in range(27):
        taps[t] = jnp.broadcast_to(0.5 * taps_ref[t : t + 1, :], taps.shape[1:]).astype(BF16)
    aug[:slices, :] = aff_ref[...].T
    aug[slices:, :] = jnp.broadcast_to(soft_ref[...], (aug.shape[0] - slices, channels)).astype(BF16)
    for copy in loads[:3]:
        copy.wait()

    def where(s):
        i, part = s // per_plane, lax.rem(s, per_plane)
        p = jnp.where(i < planes - 2, i + 1, jnp.where((i == planes - 1) == (core == 0), 0, planes - 1))
        return p, part

    first_up = jnp.where(core == 0, planes - 1, early) * per_plane
    first_down = jnp.where(core == 0, early, planes - 1) * per_plane

    def arrive(*chunks):
        @pl.when(chunks[0] == 1)
        def _():
            for copy in late:
                copy.start()

        @pl.when(chunks[-1] == min(1, planes - 1) * per_plane)
        def _():
            for copy in loads[3:]:
                copy.wait()

        @pl.when(chunks[-1] >= early * per_plane)
        def _():
            for s in chunks:
                for k in range(per_plane):

                    @pl.when(jnp.logical_and(s == first_up + k, has_left))
                    def _():
                        up[k].wait_recv()

                    @pl.when(jnp.logical_and(s == first_down + k, has_right))
                    def _():
                        down[k].wait_recv()

    def conv_unit(p, y, local, lanes, hid):
        halves = []
        for base in range(lanes.start, lanes.stop, LANES):
            cs = slice(base, base + LANES)
            v = [[pad[p + a, y + b, :, cs] for b in range(CONV_ROWS + 2)] for a in range(3)]
            rows = []
            for q in range(CONV_ROWS):
                blocks = []
                for terms in TERMS:
                    total = None
                    for a, b, c in terms:
                        tap = taps[9 * a + 3 * b + c, :, cs]
                        tap = jnp.concatenate([tap] * (rows_z // tap.shape[0]), axis=0)
                        t = tap * v[a][q + b]
                        total = t if total is None else total + t
                    blocks.append(total)
                rows.append(blocks)
            halves.append(rows)
        per = shift.shape[0] // rows_z
        for q in range(0, CONV_ROWS, per):
            operand = jnp.concatenate(
                [
                    jnp.concatenate([t for row in rows[q : q + per] for t in row], axis=0)
                    for rows in halves
                ],
                axis=1,
            )
            h = jnp.dot(shift[...], operand, preferred_element_type=F32)
            a = math.sqrt(2.0 / math.pi)
            u = h * (2 * a + (8 * a * 0.044715) * (h * h))
            hid[(local + q) * rows_z : (local + q + per) * rows_z, lanes] = (
                h + h * jnp.tanh(u)
            ).astype(BF16)

    def units(s, hid):
        if s is None:
            return [lambda: None] * 4
        p, part = where(s)
        out = []
        for local in range(0, chunk_rows, CONV_ROWS):
            for base in range(0, channels, 2 * LANES):
                out.append(
                    functools.partial(
                        conv_unit, p, part * chunk_rows + local, local, slice(base, base + 2 * LANES), hid
                    )
                )
        return out

    def soft_stages(s, hid):
        if s is None:
            return [lambda: None] * 4
        p, part = where(s)
        state = {}

        def logits():
            lt = lax.dot_general(aug[...], hid[...], (((1,), (1,)), ((), ())), preferred_element_type=F32)
            z = lt[slices : slices + 8]
            temp = 0.25 + jnp.maximum(z, 0.0) + jnp.log(1.0 + jnp.exp(-jnp.abs(z)))
            state["rate"] = LOG2E / temp
            logit[...] = lt[:slices]
            state["top"] = jnp.max(lt[:slices].reshape(slices // 8, 8, chunk), axis=0)

        def powers():
            top = jnp.broadcast_to(jnp.max(state["top"], axis=0, keepdims=True), (8, chunk))
            rate = state["rate"]
            total = None
            for j in range(0, slices, 8):
                e = jnp.exp2((logit[j : j + 8, :] - top) * rate)
                logit[j : j + 8, :] = e
                total = e if total is None else total + e
            state["sum"] = total

        def scale():
            total = jnp.sum(state["sum"], axis=0, keepdims=True)
            inverse = jnp.broadcast_to(1.0 / total, (16, chunk))
            for j in range(0, slices, 16):
                probt[j : j + 16, :] = (logit[j : j + 16, :] * inverse).astype(BF16)

        def gather():
            acc[...] += jnp.dot(probt[...], hid[...], preferred_element_type=F32)
            ones = jnp.ones((16, chunk), BF16)
            macc[...] += lax.dot_general(
                ones, probt[...], (((1,), (1,)), ((), ())), preferred_element_type=F32
            )
            rs = pl.ds(pl.multiple_of(part * chunk, chunk), chunk)
            for j in range(0, slices, LANES):
                prob[p, rs, j : j + LANES] = probt[j : j + LANES, :].T

        return [logits, powers, scale, gather]

    def step(sc, hid_c, ss, hid_s):
        for soft, conv in zip(soft_stages(ss, hid_s), units(sc, hid_c)):
            soft()
            conv()

    step(0, hid_a, None, None)

    def body(u, carry):
        arrive(2 * u + 1, 2 * u + 2)
        step(2 * u + 1, hid_b, 2 * u, hid_a)
        step(2 * u + 2, hid_a, 2 * u + 1, hid_b)
        return carry

    lax.fori_loop(0, steps // 2 - 1, body, 0)
    step(None, None, steps - 2, hid_a)
    arrive(steps - 1)
    step(steps - 1, hid_b, None, None)
    step(None, None, steps - 1, hid_b)

    def remote(src, dst, ss, rs, to):
        return pltpu.make_async_remote_copy(
            src_ref=src, dst_ref=dst, send_sem=ss, recv_sem=rs,
            device_id={"gx": to}, device_id_type=MESH,
        )

    rows = slices // n
    group = slices // count
    order = list(range(1, count)) + [0]
    lane = lax.broadcasted_iota(jnp.int32, (slices, LANES), 1)
    mass = jnp.broadcast_to(macc[:1, :], (LANES, slices)).T
    high = mass.astype(BF16).astype(F32)
    logit[:, :LANES] = jnp.where(lane < LANES // 2, high, mass - high)
    sent = []
    for d in order:
        q = ahead(d)
        rs = pl.ds(pl.multiple_of(q * group, group), group)
        g_ref[q, :, :, :, :channels] = acc[rs, :].astype(BF16).reshape(2, 2, rows, channels)
        g_ref[q, :, :, :, channels:] = logit[rs, :LANES].astype(BF16).reshape(2, 2, rows, LANES)
        copy = remote(g_ref.at[q, :, 1 - core], pair_in.at[q], s1.at[d], r1.at[d], partner)
        copy.start()
        sent.append(copy)
    pairs = dict(zip(order, sent))
    halves = {}
    for d in order:
        q = ahead(d)
        pairs[d].wait_recv()
        half_sum[q] = (g_ref[q, 1 - side, core].astype(F32) + pair_in[q, 1 - side].astype(F32)).astype(BF16)
        copy = remote(half_sum.at[q], x_in.at[q], s2.at[d], r2.at[d], beside)
        copy.start()
        halves[d] = copy
        mine[q] = g_ref[q, side, core].astype(F32) + pair_in[q, side].astype(F32)
        sent.append(copy)
    ring = {}
    for d in order[:-1]:
        q = ahead(d)
        halves[d].wait_recv()
        quarter[d] = (mine[q] + x_in[q].astype(F32)).astype(BF16)
        copy = remote(quarter.at[d], z_in.at[d], s3.at[d], r3.at[d], device(q))
        copy.start()
        ring[d] = copy
        sent.append(copy)
    halves[0].wait_recv()
    total = mine[row] + x_in[row].astype(F32)
    for copy in late:
        copy.wait()
    for d in order[:-1]:
        ring[d].wait_recv()
        total = total + z_in[d].astype(F32)

    mass = total[:, channels : channels + 1] + total[
        :, channels + LANES // 2 : channels + LANES // 2 + 1
    ]
    mean_hidden = total[:, :channels] / (mass + epsilon)
    high = mean_hidden.astype(BF16)
    low = (mean_hidden - high.astype(F32)).astype(BF16)
    tokens = jnp.dot(high, wc[...], preferred_element_type=F32) + jnp.dot(
        low, wc[...], preferred_element_type=F32
    )
    center = jnp.mean(tokens, axis=-1, keepdims=True)
    spread = jnp.mean((tokens - center) ** 2, axis=-1, keepdims=True)
    normed = ((tokens - center) * (1.0 / jnp.sqrt(spread + epsilon)) * gain_ref[...]).astype(BF16)
    inner = gelu(jnp.dot(normed, w1[...], preferred_element_type=F32)).astype(BF16)
    own = (tokens + jnp.dot(inner, w2[...], preferred_element_type=F32)).astype(BF16)
    own_ref[...] = own
    all_ref[me] = jnp.dot(own, wf[...], preferred_element_type=F32).astype(BF16)

    def give(block, ss, rs, i, to):
        copy = remote(all_ref.at[block], all_ref.at[block], ss.at[i], rs.at[i], to)
        copy.start()
        sent.append(copy)
        return copy

    along = [give(me, s4, r4, d, device(ahead(d))) for d in range(1, count)]
    across = [give(me, s5, r5, 0, beside)]
    inside_chip = [give(me, s6, r6, 0, partner)]
    for d in range(1, count):
        along[d - 1].wait_recv()
        across.append(give(device(behind(d)), s5, r5, d, beside))
        inside_chip.append(give(device(behind(d)), s6, r6, d, partner))
    for d in range(count):
        across[d].wait_recv()
        block = device(behind(d)) + 2 - 4 * side
        inside_chip.append(give(block, s6, r6, count + d, partner))
    for copy in inside_chip:
        copy.wait_recv()
    for copy in sent:
        copy.wait_send()

    @pl.when(has_right)
    def _():
        for copy in up:
            copy.wait_send()

    @pl.when(has_left)
    def _():
        for copy in down:
            copy.wait_send()


def slab(n, x, taps, aff, soft, gain, wc, w1, w2, wf):
    planes, rows_y, rows_z, channels = x.shape
    slices = aff.shape[1]
    rows, count, width = slices // n, n // 4, channels + LANES
    cells = rows_y * rows_z
    chunk = CHUNK_ROWS * rows_z
    depth = len(OFFSETS) * rows_z
    per_plane = rows_y // CHUNK_ROWS
    per = max(256 // depth, 1)
    vmem_spec = pl.BlockSpec(memory_space=pltpu.VMEM)
    dma = pltpu.SemaphoreType.DMA
    return pl.pallas_call(
        functools.partial(slab_kernel, n),
        out_shape=(
            jax.ShapeDtypeStruct((planes, cells, slices), BF16),
            jax.ShapeDtypeStruct(x.shape, BF16),
            jax.ShapeDtypeStruct((rows, channels), BF16),
            jax.ShapeDtypeStruct((n, rows, channels), BF16),
        ),
        in_specs=[pl.BlockSpec(memory_space=pltpu.HBM)] * 9,
        out_specs=(vmem_spec,) * 4,
        scratch_shapes=[
            pltpu.VMEM(taps.shape, F32),
            pltpu.VMEM(aff.shape, BF16),
            pltpu.VMEM(soft.shape, F32),
            pltpu.VMEM((planes + 2, rows_y + 2, rows_z, channels), BF16),
            pltpu.VMEM((27, 16, channels), BF16),
            pltpu.VMEM((slices + 16, channels), BF16),
            pltpu.VMEM((per * rows_z, per * depth), BF16),
            pltpu.VMEM((chunk, channels), BF16),
            pltpu.VMEM((chunk, channels), BF16),
            pltpu.VMEM((slices, chunk), F32),
            pltpu.VMEM((slices, chunk), BF16),
            pltpu.VMEM((slices, channels), F32),
            pltpu.VMEM((16, slices), F32),
            pltpu.VMEM(gain.shape, F32),
            pltpu.VMEM(wc.shape, BF16),
            pltpu.VMEM(w1.shape, BF16),
            pltpu.VMEM(w2.shape, BF16),
            pltpu.VMEM(wf.shape, BF16),
            pltpu.VMEM((count, 2, 2, rows, width), BF16),
            pltpu.VMEM((count, 2, rows, width), BF16),
            pltpu.VMEM((count, rows, width), BF16),
            pltpu.VMEM((count, rows, width), F32),
            pltpu.VMEM((count, rows, width), BF16),
            pltpu.VMEM((count, rows, width), BF16),
            pltpu.VMEM((count, rows, width), BF16),
            dma((planes,)),
            dma((3,)),
            dma((6,)),
            dma((2, per_plane)),
            dma((2, per_plane)),
        ]
        + [dma((count,))] * 10
        + [dma((2 * count,))] * 2,
        compiler_params=pltpu.CompilerParams(
            collective_id=1, has_side_effects=True, vmem_limit_bytes=SLAB_LIMIT
        ),
        name="slab",
    )(x, taps, aff, soft, gain, wc, w1, w2, wf)


def final_kernel(x_ref, p_ref, f_ref, own_ref, o_hbm, own_out, buf, sem):
    own_out[...] = own_ref[...]
    slots, block, _ = buf.shape
    steps = x_ref.shape[0] // block
    out = []
    for i in range(steps):
        rs = pl.ds(i * block, block)
        if i >= slots:
            out[i - slots].wait()
        buf[i % slots] = (
            x_ref[rs, :].astype(F32)
            + jnp.dot(p_ref[rs, :], f_ref[...], preferred_element_type=F32)
        ).astype(BF16)
        copy = pltpu.make_async_copy(buf.at[i % slots], o_hbm.at[rs, :], sem.at[i % slots])
        copy.start()
        out.append(copy)
    for copy in out[max(steps - slots, 0) :]:
        copy.wait()


def final(x, p, f, own):
    cells, channels = x.shape
    block = math.gcd(cells, 512)
    vmem_spec = pl.BlockSpec(memory_space=pltpu.VMEM)
    return pl.pallas_call(
        final_kernel,
        out_shape=(
            jax.ShapeDtypeStruct((cells, channels), BF16),
            jax.ShapeDtypeStruct(own.shape, BF16),
        ),
        in_specs=[vmem_spec] * 4,
        out_specs=(pl.BlockSpec(memory_space=pl.ANY), vmem_spec),
        scratch_shapes=[
            pltpu.VMEM((3, block, channels), BF16),
            pltpu.SemaphoreType.DMA((3,)),
        ],
        compiler_params=pltpu.CompilerParams(vmem_limit_bytes=SMALL_LIMIT),
        name="final",
    )(x, p, f, own)


def per_device(x, stencil, aff, softness, wc, gain, w1, w2, wf):
    planes, rows_y, rows_z, channels = x.shape
    n = lax.axis_size("gx")
    def held(v):
        return pltpu.with_memory_space_constraint(v, pltpu.HBM)

    probs, kept, own, folded = slab(
        n, held(x), held(stencil), held(aff), held(softness.reshape(1, -1)),
        held(gain.reshape(1, -1)), held(wc), held(w1), held(w2), held(wf),
    )
    updated, own = final(
        kept.reshape(-1, channels),
        probs.reshape(planes * rows_y * rows_z, -1),
        folded.reshape(-1, channels),
        own,
    )
    return updated.reshape(x.shape), own


def solution(mesh):
    return jax.shard_map(
        per_device,
        mesh=mesh,
        in_specs=(P(("grp", "gx"), None, None, None), P(), P(), P(), P(), P(), P(), P(), P()),
        out_specs=(P(("grp", "gx"), None, None, None), P(("grp", "gx"), None)),
        check_vma=False,
    )
```

```python
import functools
import math

import jax
import jax.numpy as jnp
from jax import lax
from jax.experimental import pallas as pl
from jax.experimental.pallas import tpu as pltpu
from jax.sharding import PartitionSpec as P

epsilon = 1e-05
MESH = pl.DeviceIdType.MESH
F32 = jnp.float32
BF16 = jnp.bfloat16
LANES = 128
MIB = 1024 * 1024
SLAB_LIMIT = 32 * MIB
SMALL_LIMIT = 16 * MIB
OFFSETS = (-1, -1, -1, 1, 1, 1, 0, 0)
TERMS = (
    [[(a, b, 0) for b in range(3)] for a in range(3)]
    + [[(a, b, 2) for b in range(3)] for a in range(3)]
    + [[(a, b, 1) for a in range(2) for b in range(3)], [(2, b, 1) for b in range(3)]]
)


def gelu(v):
    a = math.sqrt(2.0 / math.pi)
    return 0.5 * v * (1.0 + jnp.tanh(v * (a + (a * 0.044715) * (v * v))))


CONV_ROWS = 4
CHUNK_ROWS = 8
LOG2E = math.log2(math.e)


def slab_kernel(
    n, x_ref, taps_hbm, aff_hbm, soft_hbm, gain_hbm, wc_hbm, w1_hbm, w2_hbm, wf_hbm,
    prob, x_keep, own_ref, all_ref,
    taps_ref, aff_ref, soft_ref, pad, taps, aug, shift, hid_a, hid_b, logit, probt, acc, macc,
    gain_ref, wc, w1, w2, wf, g_ref, pair_in, half_sum, mine, x_in, quarter, z_in,
    load_sem, small_sem, late_sem, send_sem, recv_sem, s1, r1, s2, r2, s3, r3, s4, r4, s5, r5, s6, r6,
):
    planes, rows_y, rows_z, channels = x_ref.shape
    slices = aff_ref.shape[1]
    chunk_rows = CHUNK_ROWS
    chunk = chunk_rows * rows_z
    per_plane = rows_y // chunk_rows
    steps = planes * per_plane
    me = lax.axis_index("gx")
    inside = pl.ds(1, rows_y)
    has_left, has_right = me > 0, me < n - 1
    core, early = lax.rem(me, 2), max(planes - 2, 0)

    count = n // 4
    row, side = me // 4, lax.rem(me // 2, 2)
    partner = me + 1 - 2 * core
    beside = me + 2 - 4 * side

    def ahead(d):
        return lax.rem(row + d, count)

    def behind(d):
        return lax.rem(row + count - d, count)

    def device(q):
        return (2 * q + side) * 2 + core

    barrier = pltpu.get_barrier_semaphore()

    @pl.when(has_left)
    def _():
        pl.semaphore_signal(barrier, inc=1, device_id={"gx": me - 1}, device_id_type=MESH)

    @pl.when(has_right)
    def _():
        pl.semaphore_signal(barrier, inc=1, device_id={"gx": me + 1}, device_id_type=MESH)

    pl.semaphore_signal(barrier, inc=1, device_id={"gx": beside}, device_id_type=MESH)
    for d in range(1, count):
        pl.semaphore_signal(barrier, inc=1, device_id={"gx": device(ahead(d))}, device_id_type=MESH)

    small = []
    for i, (src, dst) in enumerate(
        ((taps_hbm, taps_ref), (aff_hbm, aff_ref), (soft_hbm, soft_ref))
    ):
        copy = pltpu.make_async_copy(src, dst, small_sem.at[i])
        copy.start()
        small.append(copy)
    loads = []
    for j in range(planes):
        copy = pltpu.make_async_copy(x_ref.at[j], pad.at[j + 1, inside], load_sem.at[j])
        copy.start()
        loads.append(copy)
    late = [
        pltpu.make_async_copy(src, dst, late_sem.at[i])
        for i, (src, dst) in enumerate(
            ((x_ref, x_keep), (wc_hbm, wc), (w1_hbm, w1), (w2_hbm, w2), (wf_hbm, wf), (gain_hbm, gain_ref))
        )
    ]

    pl.semaphore_wait(barrier, jnp.minimum(me, 1) + jnp.minimum(n - 1 - me, 1) + count)

    ends = [min((k + 1) * chunk_rows + 1, rows_y) for k in range(per_plane)]
    up, down = [], []
    for k, (lo, hi) in enumerate(zip([0] + ends[:-1], ends)):
        up.append(
            pltpu.make_async_remote_copy(
                src_ref=x_ref.at[planes - 1, pl.ds(lo, hi - lo)],
                dst_ref=pad.at[0, pl.ds(1 + lo, hi - lo)],
                send_sem=send_sem.at[0, k], recv_sem=recv_sem.at[0, k],
                device_id={"gx": me + 1}, device_id_type=MESH,
            )
        )
        down.append(
            pltpu.make_async_remote_copy(
                src_ref=x_ref.at[0, pl.ds(lo, hi - lo)],
                dst_ref=pad.at[planes + 1, pl.ds(1 + lo, hi - lo)],
                send_sem=send_sem.at[1, k], recv_sem=recv_sem.at[1, k],
                device_id={"gx": me - 1}, device_id_type=MESH,
            )
        )

    @pl.when(has_right)
    def _():
        for copy in up:
            copy.start()

    @pl.when(has_left)
    def _():
        for copy in down:
            copy.start()

    for i in range(planes + 2):
        pad[i, 0] = jnp.zeros((rows_z, channels), BF16)
        pad[i, rows_y + 1] = jnp.zeros((rows_z, channels), BF16)

    @pl.when(jnp.logical_not(has_left))
    def _():
        pad[0, inside] = jnp.zeros((rows_y, rows_z, channels), BF16)

    @pl.when(jnp.logical_not(has_right))
    def _():
        pad[planes + 1, inside] = jnp.zeros((rows_y, rows_z, channels), BF16)

    acc[...] = jnp.zeros_like(acc)
    macc[...] = jnp.zeros_like(macc)
    r = lax.broadcasted_iota(jnp.int32, shift.shape, 0)
    k = lax.broadcasted_iota(jnp.int32, shift.shape, 1)
    block = lax.rem(k // rows_z, len(OFFSETS))
    off = jnp.zeros_like(k)
    for j, o in enumerate(OFFSETS):
        off = jnp.where(block == j, o, off)
    hit = jnp.logical_and(
        k // (rows_z * len(OFFSETS)) == r // rows_z,
        lax.rem(k, rows_z) == lax.rem(r, rows_z) + off,
    )
    shift[...] = jnp.where(hit, 1.0, 0.0).astype(BF16)
    for copy in small:
        copy.wait()
    for t in range(27):
        taps[t] = jnp.broadcast_to(0.5 * taps_ref[t : t + 1, :], taps.shape[1:]).astype(BF16)
    aug[:slices, :] = aff_ref[...].T
    aug[slices:, :] = jnp.broadcast_to(soft_ref[...], (aug.shape[0] - slices, channels)).astype(BF16)
    for copy in loads[:3]:
        copy.wait()

    def where(s):
        i, part = s // per_plane, lax.rem(s, per_plane)
        p = jnp.where(i < planes - 2, i + 1, jnp.where((i == planes - 1) == (core == 0), 0, planes - 1))
        return p, part

    first_up = jnp.where(core == 0, planes - 1, early) * per_plane
    first_down = jnp.where(core == 0, early, planes - 1) * per_plane

    def arrive(*chunks):
        @pl.when(chunks[0] == 1)
        def _():
            for copy in late:
                copy.start()

        @pl.when(chunks[-1] == min(1, planes - 1) * per_plane)
        def _():
            for copy in loads[3:]:
                copy.wait()

        @pl.when(chunks[-1] >= early * per_plane)
        def _():
            for s in chunks:
                for k in range(per_plane):

                    @pl.when(jnp.logical_and(s == first_up + k, has_left))
                    def _():
                        up[k].wait_recv()

                    @pl.when(jnp.logical_and(s == first_down + k, has_right))
                    def _():
                        down[k].wait_recv()

    def conv_unit(p, y, local, lanes, hid):
        halves = []
        for base in range(lanes.start, lanes.stop, LANES):
            cs = slice(base, base + LANES)
            v = [[pad[p + a, y + b, :, cs] for b in range(CONV_ROWS + 2)] for a in range(3)]
            rows = []
            for q in range(CONV_ROWS):
                blocks = []
                for terms in TERMS:
                    total = None
                    for a, b, c in terms:
                        tap = taps[9 * a + 3 * b + c, :, cs]
                        tap = jnp.concatenate([tap] * (rows_z // tap.shape[0]), axis=0)
                        t = tap * v[a][q + b]
                        total = t if total is None else total + t
                    blocks.append(total)
                rows.append(blocks)
            halves.append(rows)
        per = shift.shape[0] // rows_z
        for q in range(0, CONV_ROWS, per):
            operand = jnp.concatenate(
                [
                    jnp.concatenate([t for row in rows[q : q + per] for t in row], axis=0)
                    for rows in halves
                ],
                axis=1,
            )
            h = jnp.dot(shift[...], operand, preferred_element_type=F32)
            a = math.sqrt(2.0 / math.pi)
            u = h * (2 * a + (8 * a * 0.044715) * (h * h))
            hid[(local + q) * rows_z : (local + q + per) * rows_z, lanes] = (
                h + h * jnp.tanh(u)
            ).astype(BF16)

    def units(s, hid):
        if s is None:
            return [lambda: None] * 4
        p, part = where(s)
        out = []
        for local in range(0, chunk_rows, CONV_ROWS):
            for base in range(0, channels, 2 * LANES):
                out.append(
                    functools.partial(
                        conv_unit, p, part * chunk_rows + local, local, slice(base, base + 2 * LANES), hid
                    )
                )
        return out

    def soft_stages(s, hid):
        if s is None:
            return [lambda: None] * 4
        p, part = where(s)
        state = {}

        def logits():
            lt = lax.dot_general(aug[...], hid[...], (((1,), (1,)), ((), ())), preferred_element_type=F32)
            z = lt[slices : slices + 8]
            temp = 0.25 + jnp.maximum(z, 0.0) + jnp.log(1.0 + jnp.exp(-jnp.abs(z)))
            state["rate"] = LOG2E / temp
            logit[...] = lt[:slices]
            state["top"] = jnp.max(lt[:slices].reshape(slices // 8, 8, chunk), axis=0)

        def powers():
            top = jnp.broadcast_to(jnp.max(state["top"], axis=0, keepdims=True), (8, chunk))
            rate = state["rate"]
            total = None
            for j in range(0, slices, 8):
                e = jnp.exp2((logit[j : j + 8, :] - top) * rate)
                logit[j : j + 8, :] = e
                total = e if total is None else total + e
            state["sum"] = total

        def scale():
            total = jnp.sum(state["sum"], axis=0, keepdims=True)
            inverse = jnp.broadcast_to(1.0 / total, (16, chunk))
            for j in range(0, slices, 16):
                probt[j : j + 16, :] = (logit[j : j + 16, :] * inverse).astype(BF16)

        def gather():
            acc[...] += jnp.dot(probt[...], hid[...], preferred_element_type=F32)
            ones = jnp.ones((16, chunk), BF16)
            macc[...] += lax.dot_general(
                ones, probt[...], (((1,), (1,)), ((), ())), preferred_element_type=F32
            )
            rs = pl.ds(pl.multiple_of(part * chunk, chunk), chunk)
            for j in range(0, slices, LANES):
                prob[p, rs, j : j + LANES] = probt[j : j + LANES, :].T

        return [logits, powers, scale, gather]

    def step(sc, hid_c, ss, hid_s):
        for soft, conv in zip(soft_stages(ss, hid_s), units(sc, hid_c)):
            soft()
            conv()

    step(0, hid_a, None, None)

    def body(u, carry):
        arrive(2 * u + 1, 2 * u + 2)
        step(2 * u + 1, hid_b, 2 * u, hid_a)
        step(2 * u + 2, hid_a, 2 * u + 1, hid_b)
        return carry

    lax.fori_loop(0, steps // 2 - 1, body, 0)
    arrive(steps - 1)
    step(steps - 1, hid_b, steps - 2, hid_a)
    step(None, None, steps - 1, hid_b)

    def remote(src, dst, ss, rs, to):
        return pltpu.make_async_remote_copy(
            src_ref=src, dst_ref=dst, send_sem=ss, recv_sem=rs,
            device_id={"gx": to}, device_id_type=MESH,
        )

    rows = slices // n
    group = slices // count
    order = list(range(1, count)) + [0]
    lane = lax.broadcasted_iota(jnp.int32, (slices, LANES), 1)
    mass = jnp.broadcast_to(macc[:1, :], (LANES, slices)).T
    high = mass.astype(BF16).astype(F32)
    logit[:, :LANES] = jnp.where(lane < LANES // 2, high, mass - high)
    sent = []
    for d in order:
        q = ahead(d)
        rs = pl.ds(pl.multiple_of(q * group, group), group)
        g_ref[q, :, :, :, :channels] = acc[rs, :].astype(BF16).reshape(2, 2, rows, channels)
        g_ref[q, :, :, :, channels:] = logit[rs, :LANES].astype(BF16).reshape(2, 2, rows, LANES)
        copy = remote(g_ref.at[q, :, 1 - core], pair_in.at[q], s1.at[d], r1.at[d], partner)
        copy.start()
        sent.append(copy)
    pairs = dict(zip(order, sent))
    halves = {}
    for d in order:
        q = ahead(d)
        pairs[d].wait_recv()
        half_sum[q] = (g_ref[q, 1 - side, core].astype(F32) + pair_in[q, 1 - side].astype(F32)).astype(BF16)
        copy = remote(half_sum.at[q], x_in.at[q], s2.at[d], r2.at[d], beside)
        copy.start()
        halves[d] = copy
        mine[q] = g_ref[q, side, core].astype(F32) + pair_in[q, side].astype(F32)
        sent.append(copy)
    ring = {}
    for d in order[:-1]:
        q = ahead(d)
        halves[d].wait_recv()
        quarter[d] = (mine[q] + x_in[q].astype(F32)).astype(BF16)
        copy = remote(quarter.at[d], z_in.at[d], s3.at[d], r3.at[d], device(q))
        copy.start()
        ring[d] = copy
        sent.append(copy)
    halves[0].wait_recv()
    total = mine[row] + x_in[row].astype(F32)
    for copy in late:
        copy.wait()
    for d in order[:-1]:
        ring[d].wait_recv()
        total = total + z_in[d].astype(F32)

    mass = total[:, channels : channels + 1] + total[
        :, channels + LANES // 2 : channels + LANES // 2 + 1
    ]
    mean_hidden = total[:, :channels] / (mass + epsilon)
    high = mean_hidden.astype(BF16)
    low = (mean_hidden - high.astype(F32)).astype(BF16)
    tokens = jnp.dot(high, wc[...], preferred_element_type=F32) + jnp.dot(
        low, wc[...], preferred_element_type=F32
    )
    center = jnp.mean(tokens, axis=-1, keepdims=True)
    spread = jnp.mean((tokens - center) ** 2, axis=-1, keepdims=True)
    normed = ((tokens - center) * (1.0 / jnp.sqrt(spread + epsilon)) * gain_ref[...]).astype(BF16)
    inner = gelu(jnp.dot(normed, w1[...], preferred_element_type=F32)).astype(BF16)
    own = (tokens + jnp.dot(inner, w2[...], preferred_element_type=F32)).astype(BF16)
    own_ref[...] = own
    all_ref[me] = jnp.dot(own, wf[...], preferred_element_type=F32).astype(BF16)

    def give(block, ss, rs, i, to):
        copy = remote(all_ref.at[block], all_ref.at[block], ss.at[i], rs.at[i], to)
        copy.start()
        sent.append(copy)
        return copy

    along = [give(me, s4, r4, d, device(ahead(d))) for d in range(1, count)]
    across = [give(me, s5, r5, 0, beside)]
    inside_chip = [give(me, s6, r6, 0, partner)]
    for d in range(1, count):
        along[d - 1].wait_recv()
        across.append(give(device(behind(d)), s5, r5, d, beside))
        inside_chip.append(give(device(behind(d)), s6, r6, d, partner))
    for d in range(count):
        across[d].wait_recv()
        block = device(behind(d)) + 2 - 4 * side
        inside_chip.append(give(block, s6, r6, count + d, partner))
    for copy in inside_chip:
        copy.wait_recv()
    for copy in sent:
        copy.wait_send()

    @pl.when(has_right)
    def _():
        for copy in up:
            copy.wait_send()

    @pl.when(has_left)
    def _():
        for copy in down:
            copy.wait_send()


def slab(n, x, taps, aff, soft, gain, wc, w1, w2, wf):
    planes, rows_y, rows_z, channels = x.shape
    slices = aff.shape[1]
    rows, count, width = slices // n, n // 4, channels + LANES
    cells = rows_y * rows_z
    chunk = CHUNK_ROWS * rows_z
    depth = len(OFFSETS) * rows_z
    per_plane = rows_y // CHUNK_ROWS
    per = max(256 // depth, 1)
    vmem_spec = pl.BlockSpec(memory_space=pltpu.VMEM)
    dma = pltpu.SemaphoreType.DMA
    return pl.pallas_call(
        functools.partial(slab_kernel, n),
        out_shape=(
            jax.ShapeDtypeStruct((planes, cells, slices), BF16),
            jax.ShapeDtypeStruct(x.shape, BF16),
            jax.ShapeDtypeStruct((rows, channels), BF16),
            jax.ShapeDtypeStruct((n, rows, channels), BF16),
        ),
        in_specs=[pl.BlockSpec(memory_space=pltpu.HBM)] * 9,
        out_specs=(vmem_spec,) * 4,
        scratch_shapes=[
            pltpu.VMEM(taps.shape, F32),
            pltpu.VMEM(aff.shape, BF16),
            pltpu.VMEM(soft.shape, F32),
            pltpu.VMEM((planes + 2, rows_y + 2, rows_z, channels), BF16),
            pltpu.VMEM((27, 16, channels), BF16),
            pltpu.VMEM((slices + 16, channels), BF16),
            pltpu.VMEM((per * rows_z, per * depth), BF16),
            pltpu.VMEM((chunk, channels), BF16),
            pltpu.VMEM((chunk, channels), BF16),
            pltpu.VMEM((slices, chunk), F32),
            pltpu.VMEM((slices, chunk), BF16),
            pltpu.VMEM((slices, channels), F32),
            pltpu.VMEM((16, slices), F32),
            pltpu.VMEM(gain.shape, F32),
            pltpu.VMEM(wc.shape, BF16),
            pltpu.VMEM(w1.shape, BF16),
            pltpu.VMEM(w2.shape, BF16),
            pltpu.VMEM(wf.shape, BF16),
            pltpu.VMEM((count, 2, 2, rows, width), BF16),
            pltpu.VMEM((count, 2, rows, width), BF16),
            pltpu.VMEM((count, rows, width), BF16),
            pltpu.VMEM((count, rows, width), F32),
            pltpu.VMEM((count, rows, width), BF16),
            pltpu.VMEM((count, rows, width), BF16),
            pltpu.VMEM((count, rows, width), BF16),
            dma((planes,)),
            dma((3,)),
            dma((6,)),
            dma((2, per_plane)),
            dma((2, per_plane)),
        ]
        + [dma((count,))] * 10
        + [dma((2 * count,))] * 2,
        compiler_params=pltpu.CompilerParams(
            collective_id=1, has_side_effects=True, vmem_limit_bytes=SLAB_LIMIT
        ),
        name="slab",
    )(x, taps, aff, soft, gain, wc, w1, w2, wf)


def final_kernel(x_ref, p_ref, f_ref, own_ref, o_hbm, own_out, buf, sem):
    own_out[...] = own_ref[...]
    slots, block, _ = buf.shape
    steps = x_ref.shape[0] // block
    out = []
    for i in range(steps):
        rs = pl.ds(i * block, block)
        if i >= slots:
            out[i - slots].wait()
        buf[i % slots] = (
            x_ref[rs, :].astype(F32)
            + jnp.dot(p_ref[rs, :], f_ref[...], preferred_element_type=F32)
        ).astype(BF16)
        copy = pltpu.make_async_copy(buf.at[i % slots], o_hbm.at[rs, :], sem.at[i % slots])
        copy.start()
        out.append(copy)
    for copy in out[max(steps - slots, 0) :]:
        copy.wait()


def final(x, p, f, own):
    cells, channels = x.shape
    block = math.gcd(cells, 1024)
    vmem_spec = pl.BlockSpec(memory_space=pltpu.VMEM)
    return pl.pallas_call(
        final_kernel,
        out_shape=(
            jax.ShapeDtypeStruct((cells, channels), BF16),
            jax.ShapeDtypeStruct(own.shape, BF16),
        ),
        in_specs=[vmem_spec] * 4,
        out_specs=(pl.BlockSpec(memory_space=pl.ANY), vmem_spec),
        scratch_shapes=[
            pltpu.VMEM((3, block, channels), BF16),
            pltpu.SemaphoreType.DMA((3,)),
        ],
        compiler_params=pltpu.CompilerParams(vmem_limit_bytes=SMALL_LIMIT),
        name="final",
    )(x, p, f, own)


def per_device(x, stencil, aff, softness, wc, gain, w1, w2, wf):
    planes, rows_y, rows_z, channels = x.shape
    n = lax.axis_size("gx")
    def held(v):
        return pltpu.with_memory_space_constraint(v, pltpu.HBM)

    probs, kept, own, folded = slab(
        n, held(x), held(stencil), held(aff), held(softness.reshape(1, -1)),
        held(gain.reshape(1, -1)), held(wc), held(w1), held(w2), held(wf),
    )
    updated, own = final(
        kept.reshape(-1, channels),
        probs.reshape(planes * rows_y * rows_z, -1),
        folded.reshape(-1, channels),
        own,
    )
    return updated.reshape(x.shape), own


def solution(mesh):
    return jax.shard_map(
        per_device,
        mesh=mesh,
        in_specs=(P(("grp", "gx"), None, None, None), P(), P(), P(), P(), P(), P(), P(), P()),
        out_specs=(P(("grp", "gx"), None, None, None), P(("grp", "gx"), None)),
        check_vma=False,
    )
```

```python
import functools
import math

import jax
import jax.numpy as jnp
from jax import lax
from jax.experimental import pallas as pl
from jax.experimental.pallas import tpu as pltpu
from jax.sharding import PartitionSpec as P

epsilon = 1e-05
MESH = pl.DeviceIdType.MESH
F32 = jnp.float32
BF16 = jnp.bfloat16
LANES = 128
MIB = 1024 * 1024
SLAB_LIMIT = 32 * MIB
SMALL_LIMIT = 16 * MIB
OFFSETS = (-1, -1, -1, 1, 1, 1, 0, 0)
TERMS = (
    [[(a, b, 0) for b in range(3)] for a in range(3)]
    + [[(a, b, 2) for b in range(3)] for a in range(3)]
    + [[(a, b, 1) for a in range(2) for b in range(3)], [(2, b, 1) for b in range(3)]]
)


def gelu(v):
    a = math.sqrt(2.0 / math.pi)
    return 0.5 * v * (1.0 + jnp.tanh(v * (a + (a * 0.044715) * (v * v))))


CONV_ROWS = 4
CHUNK_ROWS = 8
LOG2E = math.log2(math.e)


def slab_kernel(
    n, x_ref, taps_hbm, aff_hbm, soft_hbm, gain_hbm, wc_hbm, w1_hbm, w2_hbm, wf_hbm,
    prob, x_keep, own_ref, all_ref,
    taps_ref, aff_ref, soft_ref, pad, taps, aug, shift, hid_a, hid_b, logit, probt, acc, macc,
    gain_ref, wc, w1, w2, wf, g_ref, pair_in, half_sum, mine, x_in, quarter, z_in,
    load_sem, small_sem, late_sem, send_sem, recv_sem, s1, r1, s2, r2, s3, r3, s4, r4, s5, r5, s6, r6,
):
    planes, rows_y, rows_z, channels = x_ref.shape
    slices = aff_ref.shape[1]
    chunk_rows = CHUNK_ROWS
    chunk = chunk_rows * rows_z
    per_plane = rows_y // chunk_rows
    steps = planes * per_plane
    me = lax.axis_index("gx")
    inside = pl.ds(1, rows_y)
    has_left, has_right = me > 0, me < n - 1
    core, early = lax.rem(me, 2), max(planes - 2, 0)

    count = n // 4
    row, side = me // 4, lax.rem(me // 2, 2)
    partner = me + 1 - 2 * core
    beside = me + 2 - 4 * side

    def ahead(d):
        return lax.rem(row + d, count)

    def behind(d):
        return lax.rem(row + count - d, count)

    def device(q):
        return (2 * q + side) * 2 + core

    barrier = pltpu.get_barrier_semaphore()

    @pl.when(has_left)
    def _():
        pl.semaphore_signal(barrier, inc=1, device_id={"gx": me - 1}, device_id_type=MESH)

    @pl.when(has_right)
    def _():
        pl.semaphore_signal(barrier, inc=1, device_id={"gx": me + 1}, device_id_type=MESH)

    pl.semaphore_signal(barrier, inc=1, device_id={"gx": beside}, device_id_type=MESH)
    for d in range(1, count):
        pl.semaphore_signal(barrier, inc=1, device_id={"gx": device(ahead(d))}, device_id_type=MESH)
        pl.semaphore_signal(
            barrier, inc=1, device_id={"gx": device(ahead(d)) + 2 - 4 * side}, device_id_type=MESH
        )

    small = []
    for i, (src, dst) in enumerate(
        ((taps_hbm, taps_ref), (aff_hbm, aff_ref), (soft_hbm, soft_ref))
    ):
        copy = pltpu.make_async_copy(src, dst, small_sem.at[i])
        copy.start()
        small.append(copy)
    loads = []
    for j in range(planes):
        copy = pltpu.make_async_copy(x_ref.at[j], pad.at[j + 1, inside], load_sem.at[j])
        copy.start()
        loads.append(copy)
    late = [
        pltpu.make_async_copy(src, dst, late_sem.at[i])
        for i, (src, dst) in enumerate(
            ((x_ref, x_keep), (wc_hbm, wc), (w1_hbm, w1), (w2_hbm, w2), (wf_hbm, wf), (gain_hbm, gain_ref))
        )
    ]

    pl.semaphore_wait(barrier, jnp.minimum(me, 1) + jnp.minimum(n - 1 - me, 1) + 2 * count - 1)

    ends = [min((k + 1) * chunk_rows + 1, rows_y) for k in range(per_plane)]
    up, down = [], []
    for k, (lo, hi) in enumerate(zip([0] + ends[:-1], ends)):
        up.append(
            pltpu.make_async_remote_copy(
                src_ref=x_ref.at[planes - 1, pl.ds(lo, hi - lo)],
                dst_ref=pad.at[0, pl.ds(1 + lo, hi - lo)],
                send_sem=send_sem.at[0, k], recv_sem=recv_sem.at[0, k],
                device_id={"gx": me + 1}, device_id_type=MESH,
            )
        )
        down.append(
            pltpu.make_async_remote_copy(
                src_ref=x_ref.at[0, pl.ds(lo, hi - lo)],
                dst_ref=pad.at[planes + 1, pl.ds(1 + lo, hi - lo)],
                send_sem=send_sem.at[1, k], recv_sem=recv_sem.at[1, k],
                device_id={"gx": me - 1}, device_id_type=MESH,
            )
        )

    @pl.when(has_right)
    def _():
        for copy in up:
            copy.start()

    @pl.when(has_left)
    def _():
        for copy in down:
            copy.start()

    for i in range(planes + 2):
        pad[i, 0] = jnp.zeros((rows_z, channels), BF16)
        pad[i, rows_y + 1] = jnp.zeros((rows_z, channels), BF16)

    @pl.when(jnp.logical_not(has_left))
    def _():
        pad[0, inside] = jnp.zeros((rows_y, rows_z, channels), BF16)

    @pl.when(jnp.logical_not(has_right))
    def _():
        pad[planes + 1, inside] = jnp.zeros((rows_y, rows_z, channels), BF16)

    acc[...] = jnp.zeros_like(acc)
    macc[...] = jnp.zeros_like(macc)
    r = lax.broadcasted_iota(jnp.int32, shift.shape, 0)
    k = lax.broadcasted_iota(jnp.int32, shift.shape, 1)
    block = lax.rem(k // rows_z, len(OFFSETS))
    off = jnp.zeros_like(k)
    for j, o in enumerate(OFFSETS):
        off = jnp.where(block == j, o, off)
    hit = jnp.logical_and(
        k // (rows_z * len(OFFSETS)) == r // rows_z,
        lax.rem(k, rows_z) == lax.rem(r, rows_z) + off,
    )
    shift[...] = jnp.where(hit, 1.0, 0.0).astype(BF16)
    for copy in small:
        copy.wait()
    for t in range(27):
        taps[t] = jnp.broadcast_to(0.5 * taps_ref[t : t + 1, :], taps.shape[1:]).astype(BF16)
    aug[:slices, :] = aff_ref[...].T
    aug[slices:, :] = jnp.broadcast_to(soft_ref[...], (aug.shape[0] - slices, channels)).astype(BF16)
    for copy in loads[:3]:
        copy.wait()

    def where(s):
        i, part = s // per_plane, lax.rem(s, per_plane)
        p = jnp.where(i < planes - 2, i + 1, jnp.where((i == planes - 1) == (core == 0), 0, planes - 1))
        return p, part

    first_up = jnp.where(core == 0, planes - 1, early) * per_plane
    first_down = jnp.where(core == 0, early, planes - 1) * per_plane

    def arrive(*chunks):
        @pl.when(chunks[0] == 1)
        def _():
            for copy in late:
                copy.start()

        @pl.when(chunks[-1] == min(1, planes - 1) * per_plane)
        def _():
            for copy in loads[3:]:
                copy.wait()

        @pl.when(chunks[-1] >= early * per_plane)
        def _():
            for s in chunks:
                for k in range(per_plane):

                    @pl.when(jnp.logical_and(s == first_up + k, has_left))
                    def _():
                        up[k].wait_recv()

                    @pl.when(jnp.logical_and(s == first_down + k, has_right))
                    def _():
                        down[k].wait_recv()

    def conv_unit(p, y, local, lanes, hid):
        halves = []
        for base in range(lanes.start, lanes.stop, LANES):
            cs = slice(base, base + LANES)
            v = [[pad[p + a, y + b, :, cs] for b in range(CONV_ROWS + 2)] for a in range(3)]
            rows = []
            for q in range(CONV_ROWS):
                blocks = []
                for terms in TERMS:
                    total = None
                    for a, b, c in terms:
                        tap = taps[9 * a + 3 * b + c, :, cs]
                        tap = jnp.concatenate([tap] * (rows_z // tap.shape[0]), axis=0)
                        t = tap * v[a][q + b]
                        total = t if total is None else total + t
                    blocks.append(total)
                rows.append(blocks)
            halves.append(rows)
        per = shift.shape[0] // rows_z
        for q in range(0, CONV_ROWS, per):
            operand = jnp.concatenate(
                [
                    jnp.concatenate([t for row in rows[q : q + per] for t in row], axis=0)
                    for rows in halves
                ],
                axis=1,
            )
            h = jnp.dot(shift[...], operand, preferred_element_type=F32)
            a = math.sqrt(2.0 / math.pi)
            u = h * (2 * a + (8 * a * 0.044715) * (h * h))
            hid[(local + q) * rows_z : (local + q + per) * rows_z, lanes] = (
                h + h * jnp.tanh(u)
            ).astype(BF16)

    def units(s, hid):
        if s is None:
            return [lambda: None] * 4
        p, part = where(s)
        out = []
        for local in range(0, chunk_rows, CONV_ROWS):
            for base in range(0, channels, 2 * LANES):
                out.append(
                    functools.partial(
                        conv_unit, p, part * chunk_rows + local, local, slice(base, base + 2 * LANES), hid
                    )
                )
        return out

    def soft_stages(s, hid):
        if s is None:
            return [lambda: None] * 4
        p, part = where(s)
        state = {}

        def logits():
            lt = lax.dot_general(aug[...], hid[...], (((1,), (1,)), ((), ())), preferred_element_type=F32)
            z = lt[slices : slices + 8]
            temp = 0.25 + jnp.maximum(z, 0.0) + jnp.log(1.0 + jnp.exp(-jnp.abs(z)))
            state["rate"] = LOG2E / temp
            logit[...] = lt[:slices]
            state["top"] = jnp.max(lt[:slices].reshape(slices // 8, 8, chunk), axis=0)

        def powers():
            top = jnp.broadcast_to(jnp.max(state["top"], axis=0, keepdims=True), (8, chunk))
            rate = state["rate"]
            total = None
            for j in range(0, slices, 8):
                e = jnp.exp2((logit[j : j + 8, :] - top) * rate)
                logit[j : j + 8, :] = e
                total = e if total is None else total + e
            state["sum"] = total

        def scale():
            total = jnp.sum(state["sum"], axis=0, keepdims=True)
            inverse = jnp.broadcast_to(1.0 / total, (16, chunk))
            for j in range(0, slices, 16):
                probt[j : j + 16, :] = (logit[j : j + 16, :] * inverse).astype(BF16)

        def gather():
            acc[...] += jnp.dot(probt[...], hid[...], preferred_element_type=F32)
            ones = jnp.ones((16, chunk), BF16)
            macc[...] += lax.dot_general(
                ones, probt[...], (((1,), (1,)), ((), ())), preferred_element_type=F32
            )
            rs = pl.ds(pl.multiple_of(part * chunk, chunk), chunk)
            for j in range(0, slices, LANES):
                prob[p, rs, j : j + LANES] = probt[j : j + LANES, :].T

        return [logits, powers, scale, gather]

    def step(sc, hid_c, ss, hid_s):
        for soft, conv in zip(soft_stages(ss, hid_s), units(sc, hid_c)):
            soft()
            conv()

    step(0, hid_a, None, None)

    def body(u, carry):
        arrive(2 * u + 1, 2 * u + 2)
        step(2 * u + 1, hid_b, 2 * u, hid_a)
        step(2 * u + 2, hid_a, 2 * u + 1, hid_b)
        return carry

    lax.fori_loop(0, steps // 2 - 1, body, 0)
    arrive(steps - 1)
    step(steps - 1, hid_b, steps - 2, hid_a)
    step(None, None, steps - 1, hid_b)

    def remote(src, dst, ss, rs, to):
        return pltpu.make_async_remote_copy(
            src_ref=src, dst_ref=dst, send_sem=ss, recv_sem=rs,
            device_id={"gx": to}, device_id_type=MESH,
        )

    rows = slices // n
    group = slices // count
    order = list(range(1, count)) + [0]
    lane = lax.broadcasted_iota(jnp.int32, (slices, LANES), 1)
    mass = jnp.broadcast_to(macc[:1, :], (LANES, slices)).T
    high = mass.astype(BF16).astype(F32)
    logit[:, :LANES] = jnp.where(lane < LANES // 2, high, mass - high)
    sent = []
    for d in order:
        q = ahead(d)
        rs = pl.ds(pl.multiple_of(q * group, group), group)
        g_ref[q, :, :, :, :channels] = acc[rs, :].astype(BF16).reshape(2, 2, rows, channels)
        g_ref[q, :, :, :, channels:] = logit[rs, :LANES].astype(BF16).reshape(2, 2, rows, LANES)
        copy = remote(g_ref.at[q, :, 1 - core], pair_in.at[q], s1.at[d], r1.at[d], partner)
        copy.start()
        sent.append(copy)
    pairs = dict(zip(order, sent))
    halves = {}
    for d in order:
        q = ahead(d)
        pairs[d].wait_recv()
        half_sum[q] = (g_ref[q, 1 - side, core].astype(F32) + pair_in[q, 1 - side].astype(F32)).astype(BF16)
        copy = remote(half_sum.at[q], x_in.at[q], s2.at[d], r2.at[d], beside)
        copy.start()
        halves[d] = copy
        mine[q] = g_ref[q, side, core].astype(F32) + pair_in[q, side].astype(F32)
        sent.append(copy)
    ring = {}
    for d in order[:-1]:
        q = ahead(d)
        halves[d].wait_recv()
        quarter[d] = (mine[q] + x_in[q].astype(F32)).astype(BF16)
        copy = remote(quarter.at[d], z_in.at[d], s3.at[d], r3.at[d], device(q))
        copy.start()
        ring[d] = copy
        sent.append(copy)
    halves[0].wait_recv()
    total = mine[row] + x_in[row].astype(F32)
    for copy in late:
        copy.wait()
    for d in order[:-1]:
        ring[d].wait_recv()
        total = total + z_in[d].astype(F32)

    mass = total[:, channels : channels + 1] + total[
        :, channels + LANES // 2 : channels + LANES // 2 + 1
    ]
    mean_hidden = total[:, :channels] / (mass + epsilon)
    high = mean_hidden.astype(BF16)
    low = (mean_hidden - high.astype(F32)).astype(BF16)
    tokens = jnp.dot(high, wc[...], preferred_element_type=F32) + jnp.dot(
        low, wc[...], preferred_element_type=F32
    )
    center = jnp.mean(tokens, axis=-1, keepdims=True)
    spread = jnp.mean((tokens - center) ** 2, axis=-1, keepdims=True)
    normed = ((tokens - center) * (1.0 / jnp.sqrt(spread + epsilon)) * gain_ref[...]).astype(BF16)
    inner = gelu(jnp.dot(normed, w1[...], preferred_element_type=F32)).astype(BF16)
    own = (tokens + jnp.dot(inner, w2[...], preferred_element_type=F32)).astype(BF16)
    own_ref[...] = own
    all_ref[me] = jnp.dot(own, wf[...], preferred_element_type=F32).astype(BF16)

    def give(block, ss, rs, i, to):
        copy = remote(all_ref.at[block], all_ref.at[block], ss.at[i], rs.at[i], to)
        copy.start()
        sent.append(copy)
        return copy

    across = [give(me, s5, r5, 0, beside)]
    along = []
    for d in range(1, count):
        along.append(give(me, s4, r4, d, device(ahead(d))))
        across.append(give(me, s5, r5, d, device(ahead(d)) + 2 - 4 * side))
    inside_chip = [give(me, s6, r6, 0, partner)]
    across[0].wait_recv()
    inside_chip.append(give(beside, s6, r6, count, partner))
    for d in range(1, count):
        along[d - 1].wait_recv()
        inside_chip.append(give(device(behind(d)), s6, r6, d, partner))
        across[d].wait_recv()
        inside_chip.append(give(device(behind(d)) + 2 - 4 * side, s6, r6, count + d, partner))
    for copy in inside_chip:
        copy.wait_recv()
    for copy in sent:
        copy.wait_send()

    @pl.when(has_right)
    def _():
        for copy in up:
            copy.wait_send()

    @pl.when(has_left)
    def _():
        for copy in down:
            copy.wait_send()


def slab(n, x, taps, aff, soft, gain, wc, w1, w2, wf):
    planes, rows_y, rows_z, channels = x.shape
    slices = aff.shape[1]
    rows, count, width = slices // n, n // 4, channels + LANES
    cells = rows_y * rows_z
    chunk = CHUNK_ROWS * rows_z
    depth = len(OFFSETS) * rows_z
    per_plane = rows_y // CHUNK_ROWS
    per = max(256 // depth, 1)
    vmem_spec = pl.BlockSpec(memory_space=pltpu.VMEM)
    dma = pltpu.SemaphoreType.DMA
    return pl.pallas_call(
        functools.partial(slab_kernel, n),
        out_shape=(
            jax.ShapeDtypeStruct((planes, cells, slices), BF16),
            jax.ShapeDtypeStruct(x.shape, BF16),
            jax.ShapeDtypeStruct((rows, channels), BF16),
            jax.ShapeDtypeStruct((n, rows, channels), BF16),
        ),
        in_specs=[pl.BlockSpec(memory_space=pltpu.HBM)] * 9,
        out_specs=(vmem_spec,) * 4,
        scratch_shapes=[
            pltpu.VMEM(taps.shape, F32),
            pltpu.VMEM(aff.shape, BF16),
            pltpu.VMEM(soft.shape, F32),
            pltpu.VMEM((planes + 2, rows_y + 2, rows_z, channels), BF16),
            pltpu.VMEM((27, 16, channels), BF16),
            pltpu.VMEM((slices + 16, channels), BF16),
            pltpu.VMEM((per * rows_z, per * depth), BF16),
            pltpu.VMEM((chunk, channels), BF16),
            pltpu.VMEM((chunk, channels), BF16),
            pltpu.VMEM((slices, chunk), F32),
            pltpu.VMEM((slices, chunk), BF16),
            pltpu.VMEM((slices, channels), F32),
            pltpu.VMEM((16, slices), F32),
            pltpu.VMEM(gain.shape, F32),
            pltpu.VMEM(wc.shape, BF16),
            pltpu.VMEM(w1.shape, BF16),
            pltpu.VMEM(w2.shape, BF16),
            pltpu.VMEM(wf.shape, BF16),
            pltpu.VMEM((count, 2, 2, rows, width), BF16),
            pltpu.VMEM((count, 2, rows, width), BF16),
            pltpu.VMEM((count, rows, width), BF16),
            pltpu.VMEM((count, rows, width), F32),
            pltpu.VMEM((count, rows, width), BF16),
            pltpu.VMEM((count, rows, width), BF16),
            pltpu.VMEM((count, rows, width), BF16),
            dma((planes,)),
            dma((3,)),
            dma((6,)),
            dma((2, per_plane)),
            dma((2, per_plane)),
        ]
        + [dma((count,))] * 10
        + [dma((2 * count,))] * 2,
        compiler_params=pltpu.CompilerParams(
            collective_id=1, has_side_effects=True, vmem_limit_bytes=SLAB_LIMIT
        ),
        name="slab",
    )(x, taps, aff, soft, gain, wc, w1, w2, wf)


def final_kernel(x_ref, p_ref, f_ref, own_ref, o_hbm, own_out, buf, sem):
    own_out[...] = own_ref[...]
    slots, block, _ = buf.shape
    steps = x_ref.shape[0] // block
    out = []
    for i in range(steps):
        rs = pl.ds(i * block, block)
        if i >= slots:
            out[i - slots].wait()
        buf[i % slots] = (
            x_ref[rs, :].astype(F32)
            + jnp.dot(p_ref[rs, :], f_ref[...], preferred_element_type=F32)
        ).astype(BF16)
        copy = pltpu.make_async_copy(buf.at[i % slots], o_hbm.at[rs, :], sem.at[i % slots])
        copy.start()
        out.append(copy)
    for copy in out[max(steps - slots, 0) :]:
        copy.wait()


def final(x, p, f, own):
    cells, channels = x.shape
    block = math.gcd(cells, 1024)
    vmem_spec = pl.BlockSpec(memory_space=pltpu.VMEM)
    return pl.pallas_call(
        final_kernel,
        out_shape=(
            jax.ShapeDtypeStruct((cells, channels), BF16),
            jax.ShapeDtypeStruct(own.shape, BF16),
        ),
        in_specs=[vmem_spec] * 4,
        out_specs=(pl.BlockSpec(memory_space=pl.ANY), vmem_spec),
        scratch_shapes=[
            pltpu.VMEM((3, block, channels), BF16),
            pltpu.SemaphoreType.DMA((3,)),
        ],
        compiler_params=pltpu.CompilerParams(vmem_limit_bytes=SMALL_LIMIT),
        name="final",
    )(x, p, f, own)


def per_device(x, stencil, aff, softness, wc, gain, w1, w2, wf):
    planes, rows_y, rows_z, channels = x.shape
    n = lax.axis_size("gx")
    def held(v):
        return pltpu.with_memory_space_constraint(v, pltpu.HBM)

    probs, kept, own, folded = slab(
        n, held(x), held(stencil), held(aff), held(softness.reshape(1, -1)),
        held(gain.reshape(1, -1)), held(wc), held(w1), held(w2), held(wf),
    )
    updated, own = final(
        kept.reshape(-1, channels),
        probs.reshape(planes * rows_y * rows_z, -1),
        folded.reshape(-1, channels),
        own,
    )
    return updated.reshape(x.shape), own


def solution(mesh):
    return jax.shard_map(
        per_device,
        mesh=mesh,
        in_specs=(P(("grp", "gx"), None, None, None), P(), P(), P(), P(), P(), P(), P(), P()),
        out_specs=(P(("grp", "gx"), None, None, None), P(("grp", "gx"), None)),
        check_vma=False,
    )
```

```python
import functools
import math

import jax
import jax.numpy as jnp
from jax import lax
from jax.experimental import pallas as pl
from jax.experimental.pallas import tpu as pltpu
from jax.sharding import PartitionSpec as P

epsilon = 1e-05
MESH = pl.DeviceIdType.MESH
F32 = jnp.float32
BF16 = jnp.bfloat16
LANES = 128
MIB = 1024 * 1024
SLAB_LIMIT = 32 * MIB
SMALL_LIMIT = 16 * MIB
OFFSETS = (-1, -1, -1, 1, 1, 1, 0, 0)
TERMS = (
    [[(a, b, 0) for b in range(3)] for a in range(3)]
    + [[(a, b, 2) for b in range(3)] for a in range(3)]
    + [[(a, b, 1) for a in range(2) for b in range(3)], [(2, b, 1) for b in range(3)]]
)


def gelu(v):
    a = math.sqrt(2.0 / math.pi)
    return 0.5 * v * (1.0 + jnp.tanh(v * (a + (a * 0.044715) * (v * v))))


CONV_ROWS = 4
CHUNK_ROWS = 8
LOG2E = math.log2(math.e)


def slab_kernel(
    n, x_ref, taps_hbm, aff_hbm, soft_hbm, gain_hbm, wc_hbm, w1_hbm, w2_hbm, wf_hbm,
    prob, x_keep, own_ref, all_ref,
    taps_ref, aff_ref, soft_ref, pad, taps, aug, shift, hid_a, hid_b, logit, probt, acc, macc,
    gain_ref, wc, w1, w2, wf, g_ref, pair_in, half_sum, mine, x_in, quarter, z_in,
    load_sem, small_sem, late_sem, send_sem, recv_sem, s1, r1, s2, r2, s3, r3, s4, r4, s5, r5, s6, r6,
):
    planes, rows_y, rows_z, channels = x_ref.shape
    slices = aff_ref.shape[1]
    chunk_rows = CHUNK_ROWS
    chunk = chunk_rows * rows_z
    per_plane = rows_y // chunk_rows
    steps = planes * per_plane
    me = lax.axis_index("gx")
    inside = pl.ds(1, rows_y)
    has_left, has_right = me > 0, me < n - 1
    core, early = lax.rem(me, 2), max(planes - 2, 0)

    count = n // 4
    row, side = me // 4, lax.rem(me // 2, 2)
    partner = me + 1 - 2 * core
    beside = me + 2 - 4 * side

    def ahead(d):
        return lax.rem(row + d, count)

    def behind(d):
        return lax.rem(row + count - d, count)

    def device(q):
        return (2 * q + side) * 2 + core

    barrier = pltpu.get_barrier_semaphore()

    @pl.when(has_left)
    def _():
        pl.semaphore_signal(barrier, inc=1, device_id={"gx": me - 1}, device_id_type=MESH)

    @pl.when(has_right)
    def _():
        pl.semaphore_signal(barrier, inc=1, device_id={"gx": me + 1}, device_id_type=MESH)

    pl.semaphore_signal(barrier, inc=1, device_id={"gx": beside}, device_id_type=MESH)
    for d in range(1, count):
        pl.semaphore_signal(barrier, inc=1, device_id={"gx": device(ahead(d))}, device_id_type=MESH)
        pl.semaphore_signal(
            barrier, inc=1, device_id={"gx": device(ahead(d)) + 2 - 4 * side}, device_id_type=MESH
        )

    small = []
    for i, (src, dst) in enumerate(
        ((taps_hbm, taps_ref), (aff_hbm, aff_ref), (soft_hbm, soft_ref))
    ):
        copy = pltpu.make_async_copy(src, dst, small_sem.at[i])
        copy.start()
        small.append(copy)
    loads = []
    for j in range(planes):
        copy = pltpu.make_async_copy(x_ref.at[j], pad.at[j + 1, inside], load_sem.at[j])
        copy.start()
        loads.append(copy)
    late = [
        pltpu.make_async_copy(src, dst, late_sem.at[i])
        for i, (src, dst) in enumerate(
            ((x_ref, x_keep), (wc_hbm, wc), (w1_hbm, w1), (w2_hbm, w2), (wf_hbm, wf), (gain_hbm, gain_ref))
        )
    ]

    pl.semaphore_wait(barrier, jnp.minimum(me, 1) + jnp.minimum(n - 1 - me, 1) + 2 * count - 1)

    ends = [min((k + 1) * chunk_rows + 1, rows_y) for k in range(per_plane)]
    up, down = [], []
    for k, (lo, hi) in enumerate(zip([0] + ends[:-1], ends)):
        up.append(
            pltpu.make_async_remote_copy(
                src_ref=x_ref.at[planes - 1, pl.ds(lo, hi - lo)],
                dst_ref=pad.at[0, pl.ds(1 + lo, hi - lo)],
                send_sem=send_sem.at[0, k], recv_sem=recv_sem.at[0, k],
                device_id={"gx": me + 1}, device_id_type=MESH,
            )
        )
        down.append(
            pltpu.make_async_remote_copy(
                src_ref=x_ref.at[0, pl.ds(lo, hi - lo)],
                dst_ref=pad.at[planes + 1, pl.ds(1 + lo, hi - lo)],
                send_sem=send_sem.at[1, k], recv_sem=recv_sem.at[1, k],
                device_id={"gx": me - 1}, device_id_type=MESH,
            )
        )

    @pl.when(has_right)
    def _():
        for copy in up:
            copy.start()

    @pl.when(has_left)
    def _():
        for copy in down:
            copy.start()

    for i in range(planes + 2):
        pad[i, 0] = jnp.zeros((rows_z, channels), BF16)
        pad[i, rows_y + 1] = jnp.zeros((rows_z, channels), BF16)

    @pl.when(jnp.logical_not(has_left))
    def _():
        pad[0, inside] = jnp.zeros((rows_y, rows_z, channels), BF16)

    @pl.when(jnp.logical_not(has_right))
    def _():
        pad[planes + 1, inside] = jnp.zeros((rows_y, rows_z, channels), BF16)

    acc[...] = jnp.zeros_like(acc)
    macc[...] = jnp.zeros_like(macc)
    r = lax.broadcasted_iota(jnp.int32, shift.shape, 0)
    k = lax.broadcasted_iota(jnp.int32, shift.shape, 1)
    block = lax.rem(k // rows_z, len(OFFSETS))
    off = jnp.zeros_like(k)
    for j, o in enumerate(OFFSETS):
        off = jnp.where(block == j, o, off)
    hit = jnp.logical_and(
        k // (rows_z * len(OFFSETS)) == r // rows_z,
        lax.rem(k, rows_z) == lax.rem(r, rows_z) + off,
    )
    shift[...] = jnp.where(hit, 1.0, 0.0).astype(BF16)
    for copy in small:
        copy.wait()
    for t in range(27):
        taps[t] = jnp.broadcast_to(0.5 * taps_ref[t : t + 1, :], taps.shape[1:]).astype(BF16)
    aug[:slices, :] = aff_ref[...].T
    aug[slices:, :] = jnp.broadcast_to(soft_ref[...], (aug.shape[0] - slices, channels)).astype(BF16)
    for copy in loads[:3]:
        copy.wait()

    def where(s):
        i, part = s // per_plane, lax.rem(s, per_plane)
        p = jnp.where(i < planes - 2, i + 1, jnp.where((i == planes - 1) == (core == 0), 0, planes - 1))
        return p, part

    first_up = jnp.where(core == 0, planes - 1, early) * per_plane
    first_down = jnp.where(core == 0, early, planes - 1) * per_plane

    def arrive(*chunks):
        @pl.when(chunks[0] == 1)
        def _():
            for copy in late:
                copy.start()

        @pl.when(chunks[-1] == min(1, planes - 1) * per_plane)
        def _():
            for copy in loads[3:]:
                copy.wait()

        @pl.when(chunks[-1] >= early * per_plane)
        def _():
            for s in chunks:
                for k in range(per_plane):

                    @pl.when(jnp.logical_and(s == first_up + k, has_left))
                    def _():
                        up[k].wait_recv()

                    @pl.when(jnp.logical_and(s == first_down + k, has_right))
                    def _():
                        down[k].wait_recv()

    def conv_unit(p, y, local, lanes, hid):
        halves = []
        for base in range(lanes.start, lanes.stop, LANES):
            cs = slice(base, base + LANES)
            v = [[pad[p + a, y + b, :, cs] for b in range(CONV_ROWS + 2)] for a in range(3)]
            rows = []
            for q in range(CONV_ROWS):
                blocks = []
                for terms in TERMS:
                    total = None
                    for a, b, c in terms:
                        tap = taps[9 * a + 3 * b + c, :, cs]
                        tap = jnp.concatenate([tap] * (rows_z // tap.shape[0]), axis=0)
                        t = tap * v[a][q + b]
                        total = t if total is None else total + t
                    blocks.append(total)
                rows.append(blocks)
            halves.append(rows)
        per = shift.shape[0] // rows_z
        for q in range(0, CONV_ROWS, per):
            operand = jnp.concatenate(
                [
                    jnp.concatenate([t for row in rows[q : q + per] for t in row], axis=0)
                    for rows in halves
                ],
                axis=1,
            )
            h = jnp.dot(shift[...], operand, preferred_element_type=F32)
            a = math.sqrt(2.0 / math.pi)
            u = h * (2 * a + (8 * a * 0.044715) * (h * h))
            hid[(local + q) * rows_z : (local + q + per) * rows_z, lanes] = (
                h + h * jnp.tanh(u)
            ).astype(BF16)

    def units(s, hid):
        if s is None:
            return [lambda: None] * 4
        p, part = where(s)
        out = []
        for local in range(0, chunk_rows, CONV_ROWS):
            for base in range(0, channels, 2 * LANES):
                out.append(
                    functools.partial(
                        conv_unit, p, part * chunk_rows + local, local, slice(base, base + 2 * LANES), hid
                    )
                )
        return out

    def soft_stages(s, hid):
        if s is None:
            return [lambda: None] * 4
        p, part = where(s)
        state = {}

        def logits():
            lt = lax.dot_general(aug[...], hid[...], (((1,), (1,)), ((), ())), preferred_element_type=F32)
            z = lt[slices : slices + 8]
            temp = 0.25 + jnp.maximum(z, 0.0) + jnp.log(1.0 + jnp.exp(-jnp.abs(z)))
            state["rate"] = LOG2E / temp
            logit[...] = lt[:slices]
            state["top"] = jnp.max(lt[:slices].reshape(slices // 8, 8, chunk), axis=0)

        def powers():
            top = jnp.broadcast_to(jnp.max(state["top"], axis=0, keepdims=True), (8, chunk))
            rate = state["rate"]
            total = None
            for j in range(0, slices, 8):
                e = jnp.exp2((logit[j : j + 8, :] - top) * rate)
                logit[j : j + 8, :] = e
                total = e if total is None else total + e
            state["sum"] = total

        def scale():
            total = jnp.sum(state["sum"], axis=0, keepdims=True)
            inverse = jnp.broadcast_to(1.0 / total, (16, chunk))
            for j in range(0, slices, 16):
                probt[j : j + 16, :] = (logit[j : j + 16, :] * inverse).astype(BF16)

        def gather():
            acc[...] += jnp.dot(probt[...], hid[...], preferred_element_type=F32)
            ones = jnp.ones((16, chunk), BF16)
            macc[...] += lax.dot_general(
                ones, probt[...], (((1,), (1,)), ((), ())), preferred_element_type=F32
            )
            rs = pl.ds(pl.multiple_of(part * chunk, chunk), chunk)
            for j in range(0, slices, LANES):
                prob[p, rs, j : j + LANES] = probt[j : j + LANES, :].T

        return [logits, powers, scale, gather]

    def step(sc, hid_c, ss, hid_s):
        for soft, conv in zip(soft_stages(ss, hid_s), units(sc, hid_c)):
            soft()
            conv()

    step(0, hid_a, None, None)

    def body(u, carry):
        arrive(2 * u + 1, 2 * u + 2)
        step(2 * u + 1, hid_b, 2 * u, hid_a)
        step(2 * u + 2, hid_a, 2 * u + 1, hid_b)
        return carry

    lax.fori_loop(0, steps // 2 - 1, body, 0)
    arrive(steps - 1)
    step(steps - 1, hid_b, steps - 2, hid_a)
    step(None, None, steps - 1, hid_b)

    def remote(src, dst, ss, rs, to):
        return pltpu.make_async_remote_copy(
            src_ref=src, dst_ref=dst, send_sem=ss, recv_sem=rs,
            device_id={"gx": to}, device_id_type=MESH,
        )

    rows = slices // n
    group = slices // count
    order = list(range(1, count)) + [0]
    lane = lax.broadcasted_iota(jnp.int32, (slices, LANES), 1)
    mass = jnp.broadcast_to(macc[:1, :], (LANES, slices)).T
    high = mass.astype(BF16).astype(F32)
    logit[:, :LANES] = jnp.where(lane < LANES // 2, high, mass - high)
    sent = []
    for d in order:
        q = ahead(d)
        rs = pl.ds(pl.multiple_of(q * group, group), group)
        g_ref[q, :, :, :, :channels] = acc[rs, :].astype(BF16).reshape(2, 2, rows, channels)
        g_ref[q, :, :, :, channels:] = logit[rs, :LANES].astype(BF16).reshape(2, 2, rows, LANES)
        copy = remote(g_ref.at[q, :, 1 - core], pair_in.at[q], s1.at[d], r1.at[d], partner)
        copy.start()
        sent.append(copy)
    pairs = dict(zip(order, sent))
    halves = {}
    for d in order:
        q = ahead(d)
        pairs[d].wait_recv()
        half_sum[q] = (g_ref[q, 1 - side, core].astype(F32) + pair_in[q, 1 - side].astype(F32)).astype(BF16)
        copy = remote(half_sum.at[q], x_in.at[q], s2.at[d], r2.at[d], beside)
        copy.start()
        halves[d] = copy
        mine[q] = g_ref[q, side, core].astype(F32) + pair_in[q, side].astype(F32)
        sent.append(copy)
    ring = {}
    for d in order[:-1]:
        q = ahead(d)
        halves[d].wait_recv()
        quarter[d] = (mine[q] + x_in[q].astype(F32)).astype(BF16)
        copy = remote(quarter.at[d], z_in.at[d], s3.at[d], r3.at[d], device(q))
        copy.start()
        ring[d] = copy
        sent.append(copy)
    halves[0].wait_recv()
    total = mine[row] + x_in[row].astype(F32)
    for copy in late:
        copy.wait()
    for d in order[:-1]:
        ring[d].wait_recv()
        total = total + z_in[d].astype(F32)

    mass = total[:, channels : channels + 1] + total[
        :, channels + LANES // 2 : channels + LANES // 2 + 1
    ]
    mean_hidden = total[:, :channels] / (mass + epsilon)
    high = mean_hidden.astype(BF16)
    low = (mean_hidden - high.astype(F32)).astype(BF16)
    tokens = jnp.dot(high, wc[...], preferred_element_type=F32) + jnp.dot(
        low, wc[...], preferred_element_type=F32
    )
    center = jnp.mean(tokens, axis=-1, keepdims=True)
    spread = jnp.mean((tokens - center) ** 2, axis=-1, keepdims=True)
    normed = ((tokens - center) * (1.0 / jnp.sqrt(spread + epsilon)) * gain_ref[...]).astype(BF16)
    inner = gelu(jnp.dot(normed, w1[...], preferred_element_type=F32)).astype(BF16)
    own = (tokens + jnp.dot(inner, w2[...], preferred_element_type=F32)).astype(BF16)
    own_ref[...] = own
    all_ref[me] = jnp.dot(own, wf[...], preferred_element_type=F32).astype(BF16)

    def give(block, ss, rs, i, to):
        copy = remote(all_ref.at[block], all_ref.at[block], ss.at[i], rs.at[i], to)
        copy.start()
        sent.append(copy)
        return copy

    across = [give(me, s5, r5, 0, beside)]
    along = []
    for d in range(1, count):
        along.append(give(me, s4, r4, d, device(ahead(d))))
        across.append(give(me, s5, r5, d, device(ahead(d)) + 2 - 4 * side))
    inside_chip = [give(me, s6, r6, 0, partner)]
    across[0].wait_recv()
    inside_chip.append(give(beside, s6, r6, count, partner))
    for d in range(1, count):
        along[d - 1].wait_recv()
        inside_chip.append(give(device(behind(d)), s6, r6, d, partner))
        across[d].wait_recv()
        inside_chip.append(give(device(behind(d)) + 2 - 4 * side, s6, r6, count + d, partner))
    for copy in inside_chip:
        copy.wait_recv()
    for copy in sent:
        copy.wait_send()

    @pl.when(has_right)
    def _():
        for copy in up:
            copy.wait_send()

    @pl.when(has_left)
    def _():
        for copy in down:
            copy.wait_send()


def slab(n, x, taps, aff, soft, gain, wc, w1, w2, wf):
    planes, rows_y, rows_z, channels = x.shape
    slices = aff.shape[1]
    rows, count, width = slices // n, n // 4, channels + LANES
    cells = rows_y * rows_z
    chunk = CHUNK_ROWS * rows_z
    depth = len(OFFSETS) * rows_z
    per_plane = rows_y // CHUNK_ROWS
    per = max(256 // depth, 1)
    vmem_spec = pl.BlockSpec(memory_space=pltpu.VMEM)
    dma = pltpu.SemaphoreType.DMA
    return pl.pallas_call(
        functools.partial(slab_kernel, n),
        out_shape=(
            jax.ShapeDtypeStruct((planes, cells, slices), BF16),
            jax.ShapeDtypeStruct(x.shape, BF16),
            jax.ShapeDtypeStruct((rows, channels), BF16),
            jax.ShapeDtypeStruct((n, rows, channels), BF16),
        ),
        in_specs=[pl.BlockSpec(memory_space=pltpu.HBM)] * 9,
        out_specs=(vmem_spec,) * 4,
        scratch_shapes=[
            pltpu.VMEM(taps.shape, F32),
            pltpu.VMEM(aff.shape, BF16),
            pltpu.VMEM(soft.shape, F32),
            pltpu.VMEM((planes + 2, rows_y + 2, rows_z, channels), BF16),
            pltpu.VMEM((27, 16, channels), BF16),
            pltpu.VMEM((slices + 16, channels), BF16),
            pltpu.VMEM((per * rows_z, per * depth), BF16),
            pltpu.VMEM((chunk, channels), BF16),
            pltpu.VMEM((chunk, channels), BF16),
            pltpu.VMEM((slices, chunk), F32),
            pltpu.VMEM((slices, chunk), BF16),
            pltpu.VMEM((slices, channels), F32),
            pltpu.VMEM((16, slices), F32),
            pltpu.VMEM(gain.shape, F32),
            pltpu.VMEM(wc.shape, BF16),
            pltpu.VMEM(w1.shape, BF16),
            pltpu.VMEM(w2.shape, BF16),
            pltpu.VMEM(wf.shape, BF16),
            pltpu.VMEM((count, 2, 2, rows, width), BF16),
            pltpu.VMEM((count, 2, rows, width), BF16),
            pltpu.VMEM((count, rows, width), BF16),
            pltpu.VMEM((count, rows, width), F32),
            pltpu.VMEM((count, rows, width), BF16),
            pltpu.VMEM((count, rows, width), BF16),
            pltpu.VMEM((count, rows, width), BF16),
            dma((planes,)),
            dma((3,)),
            dma((6,)),
            dma((2, per_plane)),
            dma((2, per_plane)),
        ]
        + [dma((count,))] * 10
        + [dma((2 * count,))] * 2,
        compiler_params=pltpu.CompilerParams(
            collective_id=1, has_side_effects=True, vmem_limit_bytes=SLAB_LIMIT
        ),
        name="slab",
    )(x, taps, aff, soft, gain, wc, w1, w2, wf)


def final_kernel(x_ref, p_ref, f_ref, own_ref, o_hbm, own_out, buf, sem):
    own_out[...] = own_ref[...]
    slots, block, _ = buf.shape
    steps = x_ref.shape[0] // block
    out = []
    for i in range(steps):
        rs = pl.ds(i * block, block)
        if i >= slots:
            out[i - slots].wait()
        half = x_ref.shape[1] // 2
        for cs in (slice(0, half), slice(half, 2 * half)):
            buf[i % slots, :, cs] = (
                x_ref[rs, cs].astype(F32)
                + jnp.dot(p_ref[rs, :], f_ref[:, cs], preferred_element_type=F32)
            ).astype(BF16)
        copy = pltpu.make_async_copy(buf.at[i % slots], o_hbm.at[rs, :], sem.at[i % slots])
        copy.start()
        out.append(copy)
    for copy in out[max(steps - slots, 0) :]:
        copy.wait()


def final(x, p, f, own):
    cells, channels = x.shape
    block = math.gcd(cells, 1024)
    vmem_spec = pl.BlockSpec(memory_space=pltpu.VMEM)
    return pl.pallas_call(
        final_kernel,
        out_shape=(
            jax.ShapeDtypeStruct((cells, channels), BF16),
            jax.ShapeDtypeStruct(own.shape, BF16),
        ),
        in_specs=[vmem_spec] * 4,
        out_specs=(pl.BlockSpec(memory_space=pl.ANY), vmem_spec),
        scratch_shapes=[
            pltpu.VMEM((3, block, channels), BF16),
            pltpu.SemaphoreType.DMA((3,)),
        ],
        compiler_params=pltpu.CompilerParams(vmem_limit_bytes=SMALL_LIMIT),
        name="final",
    )(x, p, f, own)


def per_device(x, stencil, aff, softness, wc, gain, w1, w2, wf):
    planes, rows_y, rows_z, channels = x.shape
    n = lax.axis_size("gx")
    def held(v):
        return pltpu.with_memory_space_constraint(v, pltpu.HBM)

    probs, kept, own, folded = slab(
        n, held(x), held(stencil), held(aff), held(softness.reshape(1, -1)),
        held(gain.reshape(1, -1)), held(wc), held(w1), held(w2), held(wf),
    )
    updated, own = final(
        kept.reshape(-1, channels),
        probs.reshape(planes * rows_y * rows_z, -1),
        folded.reshape(-1, channels),
        own,
    )
    return updated.reshape(x.shape), own


def solution(mesh):
    return jax.shard_map(
        per_device,
        mesh=mesh,
        in_specs=(P(("grp", "gx"), None, None, None), P(), P(), P(), P(), P(), P(), P(), P()),
        out_specs=(P(("grp", "gx"), None, None, None), P(("grp", "gx"), None)),
        check_vma=False,
    )
```
